32 devices in a mesh: seq: 8 (over z, core), fsdp: 4 (over y, x).
Axes of the slice: x: 2, y: 2, z: 4, core: 2. Of those that a mesh axis runs over, the one named last changes fastest.
Arguments:
- layer_inputs: bfloat16 [4, 1024, 4096], P('fsdp', 'seq'), may hold values from -8 to 8
- queries: bfloat16 [4, 1024, 4096], P('fsdp', 'seq'), may hold values from -6 to 6
- key_states: bfloat16 [4, 1024, 512], P('fsdp', 'seq'), may hold values from -4 to 4
- value_states: bfloat16 [4, 1024, 512], P('fsdp', 'seq'), may hold values from -1.75 to 1.75
- output_gradient: bfloat16 [4, 1024, 4096], P('fsdp', 'seq'), may hold values from -1.75 to 1.75
- doc_blocks: int32 [4, 4], P('fsdp'), may hold values from 1 to 3, 8 in all within a row
Outputs:
- query_grad: bfloat16 [4, 1024, 4096], P('fsdp', 'seq')
- key_grad: bfloat16 [4, 1024, 512], P('fsdp', 'seq')
- value_grad: bfloat16 [4, 1024, 512], P('fsdp', 'seq')
- value_weight_grad: bfloat16 [4096, 512], P('fsdp')
The draws below stay inside these ranges and needn't reach their ends.
Inputs may be any that keep to these rules, and one draw needn't show every extreme that they name: `doc_blocks`: the lengths of each packed row sum to 8, and each row has a document of exactly 3 blocks.
All inputs are finite; a program needn't handle non-finite values.
Results may differ from the reference program's by a relative error of at most 0.017.
Values may be sent and summed in bfloat16 or wider, within the bound.
A program may use at most 64 MiB of HBM per device.

```python
import math
import jax
import jax.numpy as jnp
import numpy as np
from jax import lax

MODEL_WIDTH = 4096
HQ = 32
KEY_VALUE_HEADS = 4
HEAD_SIZE = 128
ROWS_DEV = 128
BLOCK = 128
MOST = 3
QUERY_PER_KEY = 8
QUERY_WIDTH = 4096
KVW = 512
PACKED_ROWS = 4
PACKED_LENGTH = 1024
NBLK = 8
NDOCS = 4
BACK = 2
KEYS = 384
N_SEQ = 8


def paired_draw(key):
    base_key = jax.random.fold_in(key, 4099)
    key_q, key_k = jax.random.split(base_key, 2)
    query_vals = jnp.clip(jax.random.normal(key_q, (PACKED_ROWS, PACKED_LENGTH, QUERY_WIDTH), jnp.float32), -4.0, 4.0)
    key_vals = jnp.clip(jax.random.normal(key_k, (PACKED_ROWS, PACKED_LENGTH, KVW), jnp.float32), -4.0, 4.0)
    return (query_vals, key_vals)


def draw_queries(key, part):
    return paired_draw(key)[0].astype(jnp.bfloat16)


def draw_key_states(key, part):
    return paired_draw(key)[1].astype(jnp.bfloat16)


def raised(entries, key, source, target, shards_of, factor):
    def block_of(position):
        return (jnp.arange(entries.shape[position]) // (entries.shape[position] // shards_of)).reshape((-1,) + (1,) * (entries.ndim - 1 - position))

    near = jax.random.permutation(key, shards_of)[block_of(target)]
    other_side = (block_of(target) + shards_of // 2) % shards_of
    return jnp.where((block_of(source) == near) | (block_of(source) == other_side), factor * entries, entries)


def block_levels(key, dims, shards, low, largest):
    def one(position, shards_of):
        steps = jax.random.uniform(jax.random.fold_in(jax.random.fold_in(key, 6), position), (shards_of,), jnp.float32, low / len(shards), largest / len(shards))
        return jnp.repeat(jnp.exp(steps), dims[position] // shards_of).reshape((-1,) + (1,) * (len(dims) - position - 1))

    level = one(*shards[0])
    for cut in shards[1:]:
        level = level * one(*cut)
    return level


def length_profile(count, total, most, skew):
    loads = [(1 << 20) // math.isqrt(standing ** skew) + 1 for standing in range(2, count + 1)]
    rest, counts = total - most - (count - 1), [1] * (count - 1)
    while rest > 0:
        movable = [i for i in range(count - 1) if counts[i] < most]
        pool, budget = sum([loads[i] for i in movable]), rest
        for i in movable:
            addition = min(most - counts[i], max(1, budget * loads[i] // pool), rest)
            counts[i] = counts[i] + addition
            rest = rest - addition
    return np.array([most] + counts)


def ragged_sizes(stream_key, count, total, bound, slope):
    if count == 2:
        one = jax.random.randint(stream_key, (), max(1, total - bound), min(bound, total - 1) + 1)
        return jnp.stack([one, total - one])
    sizes = jnp.asarray(length_profile(count, total, bound, slope), jnp.int32)
    couples = (count - 1) // 2
    giver, receiver = sizes[1:1 + 2 * couples:2], sizes[2:2 + 2 * couples:2]
    margin = jnp.minimum(giver - 1, bound - receiver)
    passed = jax.random.randint(jax.random.fold_in(stream_key, 1), (couples,), 0, 1 << 20) % (margin + 1)
    sizes = sizes.at[1:1 + 2 * couples:2].set(giver - passed).at[2:2 + 2 * couples:2].set(receiver + passed)
    return sizes[jax.random.permutation(jax.random.fold_in(stream_key, 2), count)]


def scatter_about(key, shape, width, most, cuts=(), kind=jnp.bfloat16):
    loudness = block_levels(key, shape, cuts, -0.22, 0.18) if cuts else 1.0
    drawn = jax.random.normal(key, shape, jnp.float32) * width * loudness
    return jnp.minimum(jnp.maximum(drawn, -most), most).astype(kind)


def gaussian_with(key, extent, spread, limit, shards, heavy, kind=jnp.bfloat16):
    values = spread * jax.random.normal(key, extent, jnp.float32)
    if shards:
        values = values * block_levels(key, extent, shards, -0.22, 0.18)
    return jnp.clip(raised(values, jax.random.fold_in(key, 3), *heavy), -limit, limit).astype(kind)


def setup_inputs(seed: int = 0) -> dict:
    splits = jax.random.split(jax.random.key(seed), 7)
    layer_inputs = gaussian_with(splits[0], (PACKED_ROWS, PACKED_LENGTH, MODEL_WIDTH), 1.0, 8.0, ((0, 4), (1, 8)), (0, 2, 4, 2.0))
    queries = draw_queries(jax.random.fold_in(splits[6], 71), 0)
    key_states = draw_key_states(jax.random.fold_in(splits[6], 71), 0)
    value_states = scatter_about(splits[3], (PACKED_ROWS, PACKED_LENGTH, KVW), 0.3, 1.75, ((0, 4), (1, 8)))
    output_gradient = scatter_about(splits[4], (PACKED_ROWS, PACKED_LENGTH, QUERY_WIDTH), 0.3, 1.75, ((0, 4), (1, 8)))
    doc_blocks = jax.vmap(lambda own: ragged_sizes(own, NDOCS, NBLK, MOST, 2))(jax.random.split(splits[5], PACKED_ROWS)).reshape((PACKED_ROWS, NDOCS)).astype(jnp.int32)
    return {"layer_inputs": layer_inputs, "queries": queries, "key_states": key_states, "value_states": value_states, "output_gradient": output_gradient, "doc_blocks": doc_blocks}


def document_ids(positions, doc_ends):
    block_ids = jnp.floor_divide(positions, BLOCK)
    return lax.optimization_barrier(jnp.sum((block_ids[:, None] >= doc_ends[None, :]).astype(jnp.int32), axis=1))

def rounded(values_in):
    return lax.optimization_barrier(values_in.astype(jnp.bfloat16)).astype(jnp.float32)

def window_grads(query_block, gradient_block, window_keys, window_values, first_query, first_key, doc_ends):
    softmax_factor_scale = 1.0 / math.sqrt(HEAD_SIZE)
    token_rows = query_block.shape[0]
    key_number = window_keys.shape[0]
    q_pos = first_query + jnp.arange(token_rows, dtype=jnp.int32)
    k_pos = first_key + jnp.arange(key_number, dtype=jnp.int32)
    same_doc = document_ids(k_pos, doc_ends)[None, :] == document_ids(q_pos, doc_ends)[:, None]
    visible = same_doc & (k_pos[None, :] >= 0) & (k_pos[None, :] <= q_pos[:, None])
    query_head_states = query_block.astype(jnp.float32).reshape(token_rows, KEY_VALUE_HEADS, QUERY_PER_KEY, HEAD_SIZE)
    gradient_heads = gradient_block.astype(jnp.float32).reshape(token_rows, KEY_VALUE_HEADS, QUERY_PER_KEY, HEAD_SIZE)
    key_head_states = window_keys.astype(jnp.float32).reshape(key_number, KEY_VALUE_HEADS, HEAD_SIZE)
    value_head_states = window_values.astype(jnp.float32).reshape(key_number, KEY_VALUE_HEADS, HEAD_SIZE)
    scores = jnp.einsum('rghd,kgd->ghrk', query_head_states, key_head_states) * softmax_factor_scale
    scores = jnp.where(visible[None, None], scores, -jnp.inf)
    row_max = lax.optimization_barrier(jnp.max(scores, axis=-1, keepdims=True))
    exps = jnp.exp(scores - row_max)
    probs = exps / lax.optimization_barrier(jnp.sum(exps, axis=-1, keepdims=True))
    d_probs = jnp.einsum('rghd,kgd->ghrk', gradient_heads, value_head_states)
    deltas = lax.optimization_barrier(jnp.sum(probs * d_probs, axis=-1, keepdims=True))
    score_gradient = rounded(probs * (d_probs - deltas))
    probability_reduced = rounded(probs)
    value_portion = jnp.einsum('eozf,zeol->fel', probability_reduced, gradient_heads).reshape(key_number, KEY_VALUE_HEADS * HEAD_SIZE)
    key_portion = (jnp.einsum('eozf,zeol->fel', score_gradient, query_head_states) * softmax_factor_scale).reshape(key_number, KEY_VALUE_HEADS * HEAD_SIZE)
    query_portion = jnp.einsum('ghrk,kgd->rghd', score_gradient, key_head_states) * softmax_factor_scale
    return (query_portion.reshape(token_rows, KEY_VALUE_HEADS * QUERY_PER_KEY * HEAD_SIZE).astype(jnp.bfloat16), key_portion, value_portion)

def reference(layer_inputs, queries, key_states, value_states, output_gradient, doc_blocks):
    pad_rows = BACK * ROWS_DEV
    key_value_width = KEY_VALUE_HEADS * HEAD_SIZE

    def one_pack(weight_total, pack_data):
        inputs_p, queries_p, keys_p, values_p, grads_p, lengths_p = pack_data
        doc_ends = jnp.cumsum(lengths_p).astype(jnp.int32)
        zero_rows = jnp.zeros((pad_rows, key_value_width), keys_p.dtype)
        keys_pad = jnp.concatenate([zero_rows, keys_p], axis=0)
        values_pad = jnp.concatenate([zero_rows, values_p], axis=0)

        def one_shard(sums, shard_no):
            key_sum, value_sum = sums
            first_row = (shard_no * ROWS_DEV).astype(jnp.int32)
            query_block = lax.dynamic_slice_in_dim(queries_p, first_row, ROWS_DEV, 0)
            gradient_block = lax.dynamic_slice_in_dim(grads_p, first_row, ROWS_DEV, 0)
            window_keys = lax.dynamic_slice_in_dim(keys_pad, first_row, KEYS, 0)
            window_values = lax.dynamic_slice_in_dim(values_pad, first_row, KEYS, 0)
            query_portion, key_portion, value_portion = window_grads(query_block, gradient_block, window_keys, window_values, first_row, first_row - pad_rows, doc_ends)
            key_sum = lax.dynamic_update_slice_in_dim(key_sum, lax.dynamic_slice_in_dim(key_sum, first_row, KEYS, 0) + key_portion, first_row, 0)
            value_sum = lax.dynamic_update_slice_in_dim(value_sum, lax.dynamic_slice_in_dim(value_sum, first_row, KEYS, 0) + value_portion, first_row, 0)
            return ((key_sum, value_sum), query_portion)
        empty_sum = jnp.zeros((PACKED_LENGTH + pad_rows, key_value_width), jnp.float32)
        (key_sum, value_sum), query_blocks = lax.scan(one_shard, (empty_sum, empty_sum), jnp.arange(N_SEQ, dtype=jnp.int32))
        key_grad = key_sum[pad_rows:].astype(jnp.bfloat16)
        value_grad = value_sum[pad_rows:].astype(jnp.bfloat16)
        query_grad = query_blocks.reshape(PACKED_LENGTH, HQ * HEAD_SIZE)

        def one_run(total, run_pair):
            run_inputs, run_values = run_pair
            partial_w = jnp.dot(run_inputs.T, run_values, preferred_element_type=jnp.float32)
            return (total + rounded(partial_w), None)
        weight_total, _ = lax.scan(one_run, weight_total, (inputs_p.reshape(N_SEQ, ROWS_DEV, MODEL_WIDTH), value_grad.reshape(N_SEQ, ROWS_DEV, key_value_width)))
        return (weight_total, (query_grad, key_grad, value_grad))
    weight_initial = jnp.zeros((MODEL_WIDTH, KEY_VALUE_HEADS * HEAD_SIZE), jnp.float32)
    weight_total, outs_all = lax.scan(one_pack, weight_initial, (layer_inputs, queries, key_states, value_states, output_gradient, doc_blocks))
    query_grad, key_grad, value_grad = outs_all
    value_weight_grad = (weight_total / math.sqrt(PACKED_ROWS * PACKED_LENGTH)).astype(jnp.bfloat16)
    return (query_grad, key_grad, value_grad, value_weight_grad)
```

```python
import functools
import math

import jax
import jax.numpy as jnp
from jax import lax
from jax.experimental import pallas as pl
from jax.experimental.pallas import tpu as pltpu
from jax.sharding import PartitionSpec as P

HEAD_SIZE = 128
BLOCK = 128
BACK = 2
PAIR = 2
HALVES = 2
SUB = 4
SLACK = 3
VMEM_LIMIT = 40 * 1024 * 1024
SMALL_LIMIT = 8 * 1024 * 1024
MESH = pl.DeviceIdType.MESH
F32 = jnp.float32
BF16 = jnp.bfloat16


def matmul(a, b, ca, cb):
    return lax.dot_general(a, b, (((ca,), (cb,)), ((), ())), preferred_element_type=F32)


def kernel(
    n_s, n_f, groups, heads,
    doc_hbm, x_hbm, q_hbm, k_hbm, v_hbm, g_hbm,
    dq_out, dkb_out, vg_out, wfin,
    q, g, kwin, vwin, xg, probs, bias,
    dv_own, dv_send, dv_recv, dk_own, dk_send, dk_recv, vgb,
    w_own, pair_send, pair_recv, right_send, left_recv, left_send, right_recv,
    doc_ref, loc_sem, k_ss, k_rs, v_ss, v_rs, x_ss, x_rs,
    dv_ss, dv_rs, dk_ss, dk_rs, vg_ss, vg_rs, p_ss, p_rs,
    r_ss, r_rs, l_ss, l_rs, f_ss, f_rs,
):
    s = lax.axis_index("seq")
    f = lax.axis_index("fsdp")
    rows = q.shape[0]
    width = xg.shape[2]
    kvw = groups * HEAD_SIZE
    keys = (BACK + 1) * rows
    chunks = HALVES * SUB
    half_cols = kvw // HALVES
    half_rows = width // 2
    sub_rows = half_rows // SUB
    core = s % 2
    z = s // 2
    depth = n_s // 2
    sibling = s + 1 - 2 * core
    scale = 1.0 / math.sqrt(HEAD_SIZE)

    def remote(src, dst, ss, rs, to_s, to_f):
        return pltpu.make_async_remote_copy(
            src_ref=src, dst_ref=dst, send_sem=ss, recv_sem=rs,
            device_id={"seq": to_s, "fsdp": to_f}, device_id_type=MESH,
        )

    local = [
        pltpu.make_async_copy(q_hbm.at[0], q, loc_sem.at[0]),
        pltpu.make_async_copy(g_hbm.at[0], g, loc_sem.at[1]),
        pltpu.make_async_copy(k_hbm.at[0], kwin.at[BACK], loc_sem.at[2]),
        pltpu.make_async_copy(v_hbm.at[0], vwin.at[BACK], loc_sem.at[3]),
        pltpu.make_async_copy(
            x_hbm.at[0, :, pl.ds(pl.multiple_of(f * width, 128), width)], xg.at[f], loc_sem.at[4]
        ),
    ]
    doc_copy = pltpu.make_async_copy(doc_hbm, doc_ref, loc_sem.at[5])
    doc_copy.start()
    for copy in local:
        copy.start()

    barrier = pltpu.get_barrier_semaphore()
    for d in range(1, BACK + 1):
        @pl.when(s >= d)
        def _():
            pl.semaphore_signal(
                barrier, inc=1, device_id={"seq": s - d, "fsdp": f}, device_id_type=MESH
            )

        @pl.when(s + d < n_s)
        def _():
            pl.semaphore_signal(
                barrier, inc=1, device_id={"seq": s + d, "fsdp": f}, device_id_type=MESH
            )
    for j in range(1, n_f):
        pl.semaphore_signal(
            barrier, inc=1, device_id={"seq": s, "fsdp": (f + j) % n_f}, device_id_type=MESH
        )

    doc_copy.wait()

    def doc_of(block):
        end = jnp.int32(0)
        doc = jnp.int32(0)
        for i in range(doc_ref.shape[1]):
            end = end + doc_ref[0, i]
            doc = doc + jnp.where(block >= end, 1, 0)
        return doc

    mine = doc_of(s)
    for d in range(1, BACK + 1):
        seen = jnp.logical_and(doc_of(s - d) == mine, s >= d)
        level = jnp.where(seen, 0.0, -jnp.inf).astype(F32)
        bias[(BACK - d) * rows : (BACK - d + 1) * rows, :] = jnp.full(
            (rows, PAIR * rows), level, F32
        )
    key_at = lax.broadcasted_iota(jnp.int32, (rows, PAIR * rows), 0)
    query_at = lax.broadcasted_iota(jnp.int32, (rows, PAIR * rows), 1) % rows
    bias[BACK * rows :, :] = jnp.where(key_at <= query_at, 0.0, -jnp.inf).astype(F32)

    for d in range(1, BACK + 1):
        @pl.when(s < d)
        def _():
            kwin[BACK - d] = jnp.zeros((rows, kvw), BF16)
            vwin[BACK - d] = jnp.zeros((rows, kvw), BF16)

        @pl.when(s + d >= n_s)
        def _():
            dv_recv[d - 1] = jnp.zeros((rows, kvw), BF16)
            dk_recv[d - 1] = jnp.zeros((rows, kvw), BF16)

    @pl.when(z == 0)
    def _():
        left_recv[...] = jnp.zeros_like(left_recv)

    @pl.when(z == depth - 1)
    def _():
        right_recv[...] = jnp.zeros_like(right_recv)

    one = lambda c: jnp.where(c, 1, 0)
    pl.semaphore_wait(
        barrier, n_f - 1 + one(s >= 1) + one(s >= 2) + one(s + 1 < n_s) + one(s + 2 < n_s)
    )

    def group_cols(i):
        return pl.ds(pl.multiple_of(i * HEAD_SIZE, HEAD_SIZE), HEAD_SIZE)

    def k_copy(d, i):
        return remote(
            k_hbm.at[0, :, group_cols(i)], kwin.at[BACK - d, :, group_cols(i)],
            k_ss.at[d - 1, i], k_rs.at[d - 1, i], s + d, f,
        )

    def v_copy(d):
        return remote(
            v_hbm.at[0], vwin.at[BACK - d], v_ss.at[d - 1], v_rs.at[d - 1], s + d, f
        )

    def x_copy(j):
        to = (f + j) % n_f
        return remote(
            x_hbm.at[0, :, pl.ds(pl.multiple_of(to * width, 128), width)], xg.at[f],
            x_ss.at[j], x_rs.at[j], s, to,
        )

    for i in range(groups):
        for d in range(1, BACK + 1):
            @pl.when(s + d < n_s)
            def _():
                k_copy(d, i).start()
    for d in range(1, BACK + 1):
        @pl.when(s + d < n_s)
        def _():
            v_copy(d).start()
    for j in range(1, n_f):
        x_copy(j).start()

    for copy in local[:3]:
        copy.wait()

    def back_copy(send, recv, ss, rs, d, i):
        return remote(
            send.at[d - 1, :, group_cols(i)], recv.at[d - 1, :, group_cols(i)],
            ss.at[d - 1, i], rs.at[d - 1, i], s - d, f,
        )

    def pair_of(ref, i, j):
        first = (i * heads + j * PAIR) * HEAD_SIZE
        return jnp.concatenate(
            [
                ref[:, pl.ds(pl.multiple_of(first + n * HEAD_SIZE, HEAD_SIZE), HEAD_SIZE)]
                for n in range(PAIR)
            ],
            axis=0,
        )

    def give_back(total, own, send, recv, ss, rs, i):
        own[:, group_cols(i)] = total[BACK * rows :]
        for d in range(1, BACK + 1):
            send[d - 1, :, group_cols(i)] = total[(BACK - d) * rows : (BACK - d + 1) * rows].astype(
                BF16
            )

            @pl.when(s >= d)
            def _():
                back_copy(send, recv, ss, rs, d, i).start()

    def first_pass(i, carry):
        for d in range(1, BACK + 1):
            @pl.when(s >= d)
            def _():
                k_copy(d, i).wait_recv()
        k_group = kwin[:, :, group_cols(i)].reshape(keys, HEAD_SIZE)
        total = jnp.zeros((keys, HEAD_SIZE), F32)
        for j in range(heads // PAIR):
            scores = matmul(k_group, pair_of(q, i, j), 1, 1)
            scores = scores * (scale * math.log2(math.e)) + bias[...]
            exps = jnp.exp2(scores - jnp.max(scores, axis=0, keepdims=True))
            p = exps * (1.0 / jnp.sum(exps, axis=0, keepdims=True))
            probs[i, j] = p
            total = total + matmul(p.astype(BF16), pair_of(g, i, j), 1, 0)
        give_back(total, dv_own, dv_send, dv_recv, dv_ss, dv_rs, i)
        return carry

    lax.fori_loop(0, groups, first_pass, 0)

    local[3].wait()
    for d in range(1, BACK + 1):
        @pl.when(s >= d)
        def _():
            v_copy(d).wait_recv()

    def second_pass(i, carry):
        k_group = kwin[:, :, group_cols(i)].reshape(keys, HEAD_SIZE)
        v_group = vwin[:, :, group_cols(i)].reshape(keys, HEAD_SIZE)
        k_turned = k_group.T
        total = jnp.zeros((keys, HEAD_SIZE), F32)
        for j in range(heads // PAIR):
            p = probs[i, j]
            d_probs = matmul(v_group, pair_of(g, i, j), 1, 1)
            deltas = jnp.sum(p * d_probs, axis=0, keepdims=True)
            d_scores = (p * (d_probs - deltas)).astype(BF16)
            total = total + matmul(d_scores, pair_of(q, i, j), 1, 0)
            turned = (matmul(k_turned, d_scores, 1, 0) * scale).T.astype(BF16)
            first = (i * heads + j * PAIR) * HEAD_SIZE
            for n in range(PAIR):
                cols = pl.ds(pl.multiple_of(first + n * HEAD_SIZE, HEAD_SIZE), HEAD_SIZE)
                dq_out[0, :, cols] = turned[n * rows : (n + 1) * rows]
        give_back(total * scale, dk_own, dk_send, dk_recv, dk_ss, dk_rs, i)
        return carry

    def vg_copy(h, j):
        cols = pl.ds(h * half_cols, half_cols)
        return remote(
            vgb.at[f, :, cols], vgb.at[f, :, cols], vg_ss.at[h, j], vg_rs.at[h, j],
            s, (f + j) % n_f,
        )

    per_half = groups // HALVES

    def collect(own, recv, send, ss, rs, lo, count):
        for i in range(lo, lo + count):
            for d in range(1, BACK + 1):
                @pl.when(s + d < n_s)
                def _():
                    back_copy(send, recv, ss, rs, d, i).wait_recv()
        cols = slice(lo * HEAD_SIZE, (lo + count) * HEAD_SIZE)
        total = own[:, cols]
        for d in range(1, BACK + 1):
            total = total + recv[d - 1, :, cols].astype(F32)
        return total.astype(BF16)

    def value_half(h):
        cols = slice(h * half_cols, (h + 1) * half_cols)
        mine = collect(dv_own, dv_recv, dv_send, dv_ss, dv_rs, h * per_half, per_half)
        vgb[f, :, cols] = mine
        vg_out[0, :, cols] = mine
        for j in range(1, n_f):
            vg_copy(h, j).start()

    def pair_copy(h):
        return remote(
            pair_send.at[h], pair_recv.at[h], p_ss.at[h], p_rs.at[h], sibling, f
        )

    def weight_half(h):
        for j in range(1, n_f):
            vg_copy(h, j).wait_recv()
        values = vgb[:, :, h * half_cols : (h + 1) * half_cols].reshape(n_f * rows, half_cols)

        def part(which):
            lhs = xg[:, :, pl.ds(pl.multiple_of(which * half_rows, half_rows), half_rows)]
            return matmul(lhs.reshape(n_f * rows, half_rows), values, 0, 0)

        pair_send[h] = part(1 - core).astype(BF16)
        pair_copy(h).start()
        w_own[h] = part(core)

    lax.fori_loop(0, 1, second_pass, 0)
    value_half(0)
    lax.fori_loop(1, 2, second_pass, 0)
    value_half(1)
    lax.fori_loop(2, groups, second_pass, 0)
    local[4].wait()
    for j in range(1, n_f):
        x_copy(j).wait_recv()
    for h in range(HALVES):
        weight_half(h)

    def right_copy(c):
        return remote(right_send.at[c], left_recv.at[c], r_ss.at[c], r_rs.at[c], s + 2, f)

    def left_copy(c):
        return remote(left_send.at[c], right_recv.at[c], l_ss.at[c], l_rs.at[c], s - 2, f)

    def place(c, side):
        at = side * half_rows + (c % SUB) * sub_rows
        return wfin.at[
            pl.ds(pl.multiple_of(at, sub_rows), sub_rows),
            pl.ds(pl.multiple_of((c // SUB) * half_cols, half_cols), half_cols),
        ]

    def final_copy(c):
        return remote(place(c, core), place(c, core), f_ss.at[c], f_rs.at[c], sibling, f)

    def own_chunk(c):
        return w_own[c // SUB, pl.ds(pl.multiple_of((c % SUB) * sub_rows, sub_rows), sub_rows), :]

    token_count = n_f * n_s * rows

    def step(t, carry):
        to_right = t - SLACK * z
        to_left = t - SLACK * (depth - 1 - z)
        done = t - SLACK * jnp.maximum(z, depth - 1 - z)

        def inside(c):
            return jnp.logical_and(c >= 0, c < chunks)

        @pl.when(jnp.logical_and(inside(to_right), z > 0))
        def _():
            right_copy(to_right).wait_recv()

        @pl.when(jnp.logical_and(inside(to_right), z < depth - 1))
        def _():
            right_send[to_right] = (own_chunk(to_right) + left_recv[to_right].astype(F32)).astype(
                BF16
            )
            right_copy(to_right).start()

        @pl.when(jnp.logical_and(inside(to_left), z < depth - 1))
        def _():
            left_copy(to_left).wait_recv()

        @pl.when(jnp.logical_and(inside(to_left), z > 0))
        def _():
            left_send[to_left] = (own_chunk(to_left) + right_recv[to_left].astype(F32)).astype(BF16)
            left_copy(to_left).start()

        @pl.when(inside(done))
        def _():
            total = own_chunk(done) + left_recv[done].astype(F32) + right_recv[done].astype(F32)
            place(done, core)[...] = (total * (1.0 / math.sqrt(token_count))).astype(BF16)
            final_copy(done).start()

        return carry

    for h in range(HALVES):
        pair_copy(h).wait_recv()
        w_own[h] = w_own[h] + pair_recv[h].astype(F32)
        last = (h + 1) * SUB if h < HALVES - 1 else chunks + SLACK * (depth - 1)
        lax.fori_loop(h * SUB, last, step, 0)

    dkb_out[0] = collect(dk_own, dk_recv, dk_send, dk_ss, dk_rs, 0, groups)

    def settle(c, carry):
        other = remote(place(c, 1 - core), place(c, 1 - core), f_ss.at[c], f_rs.at[c], sibling, f)
        other.wait_recv()
        final_copy(c).wait_send()

        @pl.when(z < depth - 1)
        def _():
            right_copy(c).wait_send()

        @pl.when(z > 0)
        def _():
            left_copy(c).wait_send()

        return carry

    lax.fori_loop(0, chunks, settle, 0)
    for d in range(1, BACK + 1):
        @pl.when(s + d < n_s)
        def _():
            v_copy(d).wait_send()
            for i in range(groups):
                k_copy(d, i).wait_send()

        @pl.when(s >= d)
        def _():
            for i in range(groups):
                back_copy(dv_send, dv_recv, dv_ss, dv_rs, d, i).wait_send()
                back_copy(dk_send, dk_recv, dk_ss, dk_rs, d, i).wait_send()
    for j in range(1, n_f):
        x_copy(j).wait_send()
        for h in range(HALVES):
            vg_copy(h, j).wait_send()
    for h in range(HALVES):
        pair_copy(h).wait_send()


def settle_outputs(*refs):
    sources, outs, sems = refs[:4], refs[4:8], refs[8]
    saves = [pltpu.make_async_copy(sources[i], outs[i], sems.at[i]) for i in range(4)]
    for save in saves:
        save.start()
    for save in saves:
        save.wait()


def shards(n_s, n_f, layer_inputs, queries, key_states, value_states, output_gradient, doc_blocks):
    rows = queries.shape[1]
    kvw = key_states.shape[2]
    groups = kvw // HEAD_SIZE
    heads = queries.shape[2] // kvw
    width = layer_inputs.shape[2] // n_f
    chunks = HALVES * SUB
    half_cols = kvw // HALVES
    half_rows = width // 2
    sub_rows = half_rows // SUB
    keys = (BACK + 1) * rows
    V = pltpu.VMEM
    D = pltpu.SemaphoreType.DMA
    scratch = [
        V((rows, queries.shape[2]), BF16),
        V((rows, queries.shape[2]), BF16),
        V((BACK + 1, rows, kvw), BF16),
        V((BACK + 1, rows, kvw), BF16),
        V((n_f, rows, width), BF16),
        V((groups, heads // PAIR, keys, PAIR * rows), F32),
        V((keys, PAIR * rows), F32),
        V((rows, kvw), F32),
        V((BACK, rows, kvw), BF16),
        V((BACK, rows, kvw), BF16),
        V((rows, kvw), F32),
        V((BACK, rows, kvw), BF16),
        V((BACK, rows, kvw), BF16),
        V((n_f, rows, kvw), BF16),
        V((HALVES, half_rows, half_cols), F32),
        V((HALVES, half_rows, half_cols), BF16),
        V((HALVES, half_rows, half_cols), BF16),
        V((chunks, sub_rows, half_cols), BF16),
        V((chunks, sub_rows, half_cols), BF16),
        V((chunks, sub_rows, half_cols), BF16),
        V((chunks, sub_rows, half_cols), BF16),
        pltpu.SMEM(doc_blocks.shape, jnp.int32),
        D((6,)),
        D((BACK, groups)), D((BACK, groups)), D((BACK,)), D((BACK,)), D((n_f,)), D((n_f,)),
        D((BACK, groups)), D((BACK, groups)), D((BACK, groups)), D((BACK, groups)),
        D((HALVES, n_f)), D((HALVES, n_f)), D((HALVES,)), D((HALVES,)),
        D((chunks,)), D((chunks,)), D((chunks,)), D((chunks,)), D((chunks,)), D((chunks,)),
    ]
    far = pl.BlockSpec(memory_space=pltpu.HBM)
    near = pl.BlockSpec(memory_space=pltpu.VMEM)
    out_shape = [
        jax.ShapeDtypeStruct(queries.shape, BF16),
        jax.ShapeDtypeStruct(key_states.shape, BF16),
        jax.ShapeDtypeStruct(key_states.shape, BF16),
        jax.ShapeDtypeStruct((width, kvw), BF16),
    ]
    held = [
        pltpu.with_memory_space_constraint(a, pltpu.HBM)
        for a in (doc_blocks, layer_inputs, queries, key_states, value_states, output_gradient)
    ]
    made = pl.pallas_call(
        functools.partial(kernel, n_s, n_f, groups, heads),
        out_shape=[pltpu.VMEM(o.shape, o.dtype) for o in out_shape],
        in_specs=[far] * 6,
        out_specs=[near] * 4,
        scratch_shapes=scratch,
        compiler_params=pltpu.CompilerParams(
            collective_id=0, has_side_effects=True, vmem_limit_bytes=VMEM_LIMIT
        ),
    )(*held)
    return tuple(
        pl.pallas_call(
            settle_outputs,
            out_shape=out_shape,
            in_specs=[near] * 4,
            out_specs=[far] * 4,
            scratch_shapes=[D((4,))],
            compiler_params=pltpu.CompilerParams(vmem_limit_bytes=SMALL_LIMIT),
        )(*made)
    )


def solution(mesh):
    sizes = dict(mesh.shape)
    return jax.shard_map(
        functools.partial(shards, sizes["seq"], sizes["fsdp"]),
        mesh=mesh,
        in_specs=(P("fsdp", "seq", None),) * 5 + (P("fsdp", None),),
        out_specs=(P("fsdp", "seq", None),) * 3 + (P("fsdp", None),),
        check_vma=False,
    )
```

```python
import functools
import math

import jax
import jax.numpy as jnp
from jax import lax
from jax.experimental import pallas as pl
from jax.experimental.pallas import tpu as pltpu
from jax.sharding import PartitionSpec as P

HEAD_SIZE = 128
BLOCK = 128
BACK = 2
PAIR = 2
SUBS = 2
EARLY = 2
SLACK = 5
LATER = 4
AHEAD = 1
VMEM_LIMIT = 40 * 1024 * 1024
SMALL_LIMIT = 8 * 1024 * 1024
MESH = pl.DeviceIdType.MESH
F32 = jnp.float32
BF16 = jnp.bfloat16


def matmul(a, b, ca, cb):
    return lax.dot_general(a, b, (((ca,), (cb,)), ((), ())), preferred_element_type=F32)


def kernel(
    n_s, n_f, groups, heads, cuts,
    doc_hbm, x_hbm, q_hbm, k_hbm, v_hbm, g_hbm,
    dq_out, dk_out, vg_out, wfin,
    q, g, kwin, vwin, xg, probs, bias,
    dv_own, dv_send, dv_recv, dk_own, dk_send, dk_recv, vgb,
    w_own, pair_send, pair_recv, right_send, left_recv, left_send, right_recv,
    doc_ref, loc_sem, xl_sem, k_ss, k_rs, v_ss, v_rs, vr_ss, x_ss, x_rs,
    dv_ss, dv_rs, dk_ss, dk_rs, vg_ss, vg_rs, p_ss, p_rs,
    r_ss, r_rs, l_ss, l_rs, f_ss, f_rs,
):
    s = lax.axis_index("seq")
    f = lax.axis_index("fsdp")
    rows = q.shape[0]
    width = wfin.shape[0]
    cut = width // cuts
    kvw = groups * HEAD_SIZE
    keys = (BACK + 1) * rows
    couples = groups // 2
    units = cuts * couples
    chunks = units * SUBS
    sub_rows = cut // SUBS
    core = s % 2
    z = s // 2
    depth = n_s // 2
    sibling = s + 1 - 2 * core
    even = core == 0
    last = z == depth - 1
    scale = 1.0 / math.sqrt(HEAD_SIZE)

    def remote(src, dst, ss, rs, to_s, to_f):
        return pltpu.make_async_remote_copy(
            src_ref=src, dst_ref=dst, send_sem=ss, recv_sem=rs,
            device_id={"seq": to_s, "fsdp": to_f}, device_id_type=MESH,
        )

    def x_cols(to, r):
        return pl.ds(pl.multiple_of(to * width + r * cut, 128), cut)

    local = [
        pltpu.make_async_copy(q_hbm.at[0], q, loc_sem.at[0]),
        pltpu.make_async_copy(k_hbm.at[0], kwin.at[BACK], loc_sem.at[1]),
        pltpu.make_async_copy(g_hbm.at[0], g, loc_sem.at[2]),
        pltpu.make_async_copy(v_hbm.at[0], vwin.at[BACK], loc_sem.at[3]),
    ]

    def own_x(r):
        return pltpu.make_async_copy(x_hbm.at[0, :, x_cols(f, r)], xg.at[r, f], xl_sem.at[r])

    doc_copy = pltpu.make_async_copy(doc_hbm, doc_ref, loc_sem.at[4])
    doc_copy.start()
    for copy in local + [own_x(r) for r in range(cuts)]:
        copy.start()

    barrier = pltpu.get_barrier_semaphore()
    for d in range(1, BACK + 1):
        @pl.when(s >= d)
        def _():
            pl.semaphore_signal(
                barrier, inc=1, device_id={"seq": s - d, "fsdp": f}, device_id_type=MESH
            )

        @pl.when(s + d < n_s)
        def _():
            pl.semaphore_signal(
                barrier, inc=1, device_id={"seq": s + d, "fsdp": f}, device_id_type=MESH
            )
    for j in range(1, n_f):
        pl.semaphore_signal(
            barrier, inc=1, device_id={"seq": s, "fsdp": (f + j) % n_f}, device_id_type=MESH
        )

    doc_copy.wait()

    def doc_of(block):
        end = jnp.int32(0)
        doc = jnp.int32(0)
        for i in range(doc_ref.shape[1]):
            end = end + doc_ref[0, i]
            doc = doc + jnp.where(block >= end, 1, 0)
        return doc

    mine = doc_of(s)
    for d in range(1, BACK + 1):
        seen = jnp.logical_and(doc_of(s - d) == mine, s >= d)
        level = jnp.where(seen, 0.0, -jnp.inf).astype(F32)
        bias[(BACK - d) * rows : (BACK - d + 1) * rows, :] = jnp.full(
            (rows, PAIR * rows), level, F32
        )
    key_at = lax.broadcasted_iota(jnp.int32, (rows, PAIR * rows), 0)
    query_at = lax.broadcasted_iota(jnp.int32, (rows, PAIR * rows), 1) % rows
    bias[BACK * rows :, :] = jnp.where(key_at <= query_at, 0.0, -jnp.inf).astype(F32)

    for d in range(1, BACK + 1):
        @pl.when(s < d)
        def _():
            kwin[BACK - d] = jnp.zeros((rows, kvw), BF16)
            vwin[BACK - d] = jnp.zeros((rows, kvw), BF16)

        @pl.when(s + d >= n_s)
        def _():
            dv_recv[d - 1] = jnp.zeros((rows, kvw), BF16)
            dk_recv[d - 1] = jnp.zeros((rows, kvw), BF16)

    @pl.when(z == 0)
    def _():
        left_recv[...] = jnp.zeros_like(left_recv)

    @pl.when(z == depth - 1)
    def _():
        right_recv[...] = jnp.zeros_like(right_recv)

    one = lambda c: jnp.where(c, 1, 0)
    pl.semaphore_wait(
        barrier, n_f - 1 + one(s >= 1) + one(s >= 2) + one(s + 1 < n_s) + one(s + 2 < n_s)
    )

    def group_cols(i):
        return pl.ds(pl.multiple_of(i * HEAD_SIZE, HEAD_SIZE), HEAD_SIZE)

    has_next = s + 1 < n_s
    even_two = jnp.logical_and(even, s + 2 < n_s)
    relays = jnp.logical_and(even, s >= 1)

    def k_copy(d, i):
        return remote(
            k_hbm.at[0, :, group_cols(i)], kwin.at[BACK - d, :, group_cols(i)],
            k_ss.at[d - 1, i], k_rs.at[d - 1, i], s + d, f,
        )

    def v_copy(d):
        return remote(
            v_hbm.at[0], vwin.at[BACK - d], v_ss.at[d - 1], v_rs.at[d - 1], s + d, f
        )

    def v_relay():
        return remote(vwin.at[BACK - 1], vwin.at[BACK - 2], vr_ss.at[0], v_rs.at[1], s + 1, f)

    def x_copy(r, j):
        to = (f + j) % n_f
        return remote(
            x_hbm.at[0, :, x_cols(to, r)], xg.at[r, f], x_ss.at[r, j], x_rs.at[r, j], s, to
        )

    def x_start(r):
        for j in range(1, n_f):
            x_copy(r, j).start()

    for i in range(groups):
        @pl.when(has_next)
        def _():
            k_copy(1, i).start()

        @pl.when(s + 2 < n_s)
        def _():
            k_copy(2, i).start()

    @pl.when(has_next)
    def _():
        v_copy(1).start()

    @pl.when(even_two)
    def _():
        v_copy(2).start()

    for r in range(EARLY):
        x_start(r)

    for copy in local[:3]:
        copy.wait()

    def back_copy(send, recv, ss, rs, d, i):
        return remote(
            send.at[d - 1, :, group_cols(i)], recv.at[d - 1, :, group_cols(i)],
            ss.at[d - 1, i], rs.at[d - 1, i], s - d, f,
        )

    def pair_of(ref, i, j):
        first = (i * heads + j * PAIR) * HEAD_SIZE
        return jnp.concatenate(
            [
                ref[:, pl.ds(pl.multiple_of(first + n * HEAD_SIZE, HEAD_SIZE), HEAD_SIZE)]
                for n in range(PAIR)
            ],
            axis=0,
        )

    def give_back(total, own, send, recv, ss, rs, i):
        own[:, group_cols(i)] = total[BACK * rows :]
        for d in range(1, BACK + 1):
            send[d - 1, :, group_cols(i)] = total[(BACK - d) * rows : (BACK - d + 1) * rows].astype(
                BF16
            )

            @pl.when(s >= d)
            def _():
                back_copy(send, recv, ss, rs, d, i).start()

    def first_pass(i):
        @pl.when(s >= 1)
        def _():
            k_copy(1, i).wait_recv()

        @pl.when(s >= 2)
        def _():
            k_copy(2, i).wait_recv()

        k_group = kwin[:, :, group_cols(i)].reshape(keys, HEAD_SIZE)
        total = jnp.zeros((keys, HEAD_SIZE), F32)
        for j in range(heads // PAIR):
            scores = matmul(k_group, pair_of(q, i, j), 1, 1)
            scores = scores * (scale * math.log2(math.e)) + bias[...]
            exps = jnp.exp2(scores - jnp.max(scores, axis=0, keepdims=True))
            p = exps * (1.0 / jnp.sum(exps, axis=0, keepdims=True))
            probs[i, j] = p
            total = total + matmul(p.astype(BF16), pair_of(g, i, j), 1, 0)
        give_back(total, dv_own, dv_send, dv_recv, dv_ss, dv_rs, i)

    def second_pass(i):
        k_group = kwin[:, :, group_cols(i)].reshape(keys, HEAD_SIZE)
        v_group = vwin[:, :, group_cols(i)].reshape(keys, HEAD_SIZE)
        k_turned = k_group.T
        total = jnp.zeros((keys, HEAD_SIZE), F32)
        for j in range(heads // PAIR):
            p = probs[i, j]
            d_probs = matmul(v_group, pair_of(g, i, j), 1, 1)
            deltas = jnp.sum(p * d_probs, axis=0, keepdims=True)
            d_scores = (p * (d_probs - deltas)).astype(BF16)
            total = total + matmul(d_scores, pair_of(q, i, j), 1, 0)
            turned = (matmul(k_turned, d_scores, 1, 0) * scale).T.astype(BF16)
            first = (i * heads + j * PAIR) * HEAD_SIZE
            for n in range(PAIR):
                cols = pl.ds(pl.multiple_of(first + n * HEAD_SIZE, HEAD_SIZE), HEAD_SIZE)
                dq_out[0, :, cols] = turned[n * rows : (n + 1) * rows]
        give_back(total * scale, dk_own, dk_send, dk_recv, dk_ss, dk_rs, i)

    def vg_copy(i, j):
        return remote(
            vgb.at[f, :, group_cols(i)], vgb.at[f, :, group_cols(i)], vg_ss.at[i, j], vg_rs.at[i, j],
            s, (f + j) % n_f,
        )

    def collect(own, recv, send, ss, rs, i):
        for d in range(1, BACK + 1):
            @pl.when(s + d < n_s)
            def _():
                back_copy(send, recv, ss, rs, d, i).wait_recv()
        cols = group_cols(i)
        total = own[:, cols]
        for d in range(1, BACK + 1):
            total = total + recv[d - 1, :, cols].astype(F32)
        return total.astype(BF16)

    def value(i):
        done = collect(dv_own, dv_recv, dv_send, dv_ss, dv_rs, i)
        vgb[f, :, group_cols(i)] = done
        vg_out[0, :, group_cols(i)] = done
        for j in range(1, n_f):
            vg_copy(i, j).start()

    def place_of(u):
        early = u < 2 * couples
        return jnp.where(early, u % 2, u // couples), jnp.where(early, u // 2, u % couples)

    def pair_copy(u):
        return remote(pair_send.at[u], pair_recv.at[u], p_ss.at[u], p_rs.at[u], sibling, f)

    def weight_unit(u):
        r, p = place_of(jnp.int32(u))

        @pl.when(r == 0)
        def _():
            for n in range(2):
                for j in range(1, n_f):
                    vg_copy(2 * p + n, j).wait_recv()

        @pl.when(p == 0)
        def _():
            own_x(r).wait()
            for j in range(1, n_f):
                x_copy(r, j).wait_recv()

        cols = pl.ds(pl.multiple_of(2 * p * HEAD_SIZE, 2 * HEAD_SIZE), 2 * HEAD_SIZE)
        values = vgb[:, :, cols].reshape(n_f * rows, 2 * HEAD_SIZE)
        part = matmul(xg[r].reshape(n_f * rows, cut), values, 0, 0)
        first, second = part[:, :HEAD_SIZE], part[:, HEAD_SIZE:]
        w_own[u] = jnp.where(even, first, second)
        pair_send[u] = jnp.where(even, second, first).astype(BF16)
        pair_copy(u).start()

    def right_copy(c):
        return remote(right_send.at[c], left_recv.at[c], r_ss.at[c], r_rs.at[c], s + 2, f)

    def left_copy(c):
        return remote(left_send.at[c], right_recv.at[c], l_ss.at[c], l_rs.at[c], s - 2, f)

    def place(c, side):
        r, p = place_of(c // SUBS)
        at = r * cut + (c % SUBS) * sub_rows
        return wfin.at[
            pl.ds(pl.multiple_of(at, sub_rows), sub_rows), group_cols(2 * p + side)
        ]

    def final_copy(c):
        return remote(place(c, core), place(c, core), f_ss.at[c], f_rs.at[c], sibling, f)

    def own_chunk(c):
        return w_own[c // SUBS, pl.ds(pl.multiple_of((c % SUBS) * sub_rows, sub_rows), sub_rows), :]

    token_count = n_f * n_s * rows

    def step(t, carry):
        to_right = t - SLACK * z - LATER
        to_left = t - SLACK * (depth - 1 - z)
        done = jnp.minimum(to_right, to_left)

        def inside(c):
            return jnp.logical_and(c >= 0, c < chunks)

        @pl.when(jnp.logical_and(inside(to_left), z < depth - 1))
        def _():
            left_copy(to_left).wait_recv()

        @pl.when(jnp.logical_and(inside(to_left), z > 0))
        def _():
            left_send[to_left] = (own_chunk(to_left) + right_recv[to_left].astype(F32)).astype(BF16)
            left_copy(to_left).start()

        @pl.when(jnp.logical_and(inside(to_right), z > 0))
        def _():
            right_copy(to_right).wait_recv()

        @pl.when(jnp.logical_and(inside(to_right), z < depth - 1))
        def _():
            right_send[to_right] = (own_chunk(to_right) + left_recv[to_right].astype(F32)).astype(
                BF16
            )
            right_copy(to_right).start()

        @pl.when(inside(done))
        def _():
            total = own_chunk(done) + left_recv[done].astype(F32) + right_recv[done].astype(F32)
            place(done, core)[...] = (total * (1.0 / math.sqrt(token_count))).astype(BF16)
            final_copy(done).start()

        return carry

    lag = jnp.where(last, 1, 3)
    ready = groups - lag

    def first_loop(i, carry):
        @pl.when(jnp.logical_and(i >= lag, jnp.logical_not(last)))
        def _():
            value(i - lag)

        first_pass(i)

        @pl.when(jnp.logical_and(i >= lag, last))
        def _():
            value(i - lag)

        return carry

    lax.fori_loop(0, groups, first_loop, 0)

    local[3].wait()
    @pl.when(s >= 1)
    def _():
        v_copy(1).wait_recv()

    @pl.when(relays)
    def _():
        v_relay().start()

    @pl.when(s >= 2)
    def _():
        v_copy(2).wait_recv()

    early = jnp.where(last, 0, groups)

    def value_loop(k, carry):
        @pl.when(k < groups)
        def _():
            value(k)

        @pl.when(k == groups - 1)
        def _():
            for r in range(EARLY, cuts):
                x_start(r)

        @pl.when(jnp.logical_and(k >= 1, k <= early))
        def _():
            second_pass(k - 1)

        return carry

    lax.fori_loop(ready, groups + jnp.where(last, 0, 1), value_loop, 0)

    shift = jnp.minimum(SLACK * (depth - 1 - z), SLACK * z + LATER)

    def second_loop(i, carry):
        second_pass(i)
        return carry

    def line(t, carry):
        own = t - shift
        u = own // SUBS

        @pl.when(jnp.logical_and(own % SUBS == 0, jnp.logical_and(own >= 0, u + AHEAD < units)))
        def _():
            weight_unit(u + AHEAD)

        @pl.when(jnp.logical_and(own % SUBS == 0, jnp.logical_and(own >= 0, u < units)))
        def _():
            pair_copy(u).wait_recv()
            w_own[u] = w_own[u] + pair_recv[u].astype(F32)

        step(t, carry)

        @pl.when(t == chunks - 1)
        def _():
            lax.fori_loop(early, groups, second_loop, 0)

        return carry

    for u in range(AHEAD):
        weight_unit(u)
    lax.fori_loop(0, chunks + SLACK * (depth - 1) + LATER, line, 0)

    for i in range(groups):
        dk_out[0, :, i * HEAD_SIZE : (i + 1) * HEAD_SIZE] = collect(
            dk_own, dk_recv, dk_send, dk_ss, dk_rs, i
        )

    def settle(c, carry):
        other = remote(place(c, 1 - core), place(c, 1 - core), f_ss.at[c], f_rs.at[c], sibling, f)
        other.wait_recv()
        final_copy(c).wait_send()

        @pl.when(z < depth - 1)
        def _():
            right_copy(c).wait_send()

        @pl.when(z > 0)
        def _():
            left_copy(c).wait_send()

        return carry

    lax.fori_loop(0, chunks, settle, 0)

    @pl.when(has_next)
    def _():
        v_copy(1).wait_send()
        for i in range(groups):
            k_copy(1, i).wait_send()

    @pl.when(s + 2 < n_s)
    def _():
        for i in range(groups):
            k_copy(2, i).wait_send()

    @pl.when(even_two)
    def _():
        v_copy(2).wait_send()

    @pl.when(relays)
    def _():
        v_relay().wait_send()

    for d in range(1, BACK + 1):
        @pl.when(s >= d)
        def _():
            for i in range(groups):
                back_copy(dv_send, dv_recv, dv_ss, dv_rs, d, i).wait_send()
                back_copy(dk_send, dk_recv, dk_ss, dk_rs, d, i).wait_send()
    for j in range(1, n_f):
        for r in range(cuts):
            x_copy(r, j).wait_send()
        for i in range(groups):
            vg_copy(i, j).wait_send()
    for u in range(units):
        pair_copy(u).wait_send()


def settle_outputs(*refs):
    sources, outs, sems = refs[:4], refs[4:8], refs[8]
    saves = [pltpu.make_async_copy(sources[i], outs[i], sems.at[i]) for i in range(4)]
    for save in saves:
        save.start()
    for save in saves:
        save.wait()


def shards(n_s, n_f, layer_inputs, queries, key_states, value_states, output_gradient, doc_blocks):
    rows = queries.shape[1]
    kvw = key_states.shape[2]
    groups = kvw // HEAD_SIZE
    heads = queries.shape[2] // kvw
    width = layer_inputs.shape[2] // n_f
    cuts = 4 if width % (4 * 128) == 0 else 2
    cut = width // cuts
    units = cuts * (groups // 2)
    chunks = units * SUBS
    keys = (BACK + 1) * rows
    V = pltpu.VMEM
    D = pltpu.SemaphoreType.DMA
    strip = V((chunks, cut // SUBS, HEAD_SIZE), BF16)
    scratch = [
        V((rows, queries.shape[2]), BF16),
        V((rows, queries.shape[2]), BF16),
        V((BACK + 1, rows, kvw), BF16),
        V((BACK + 1, rows, kvw), BF16),
        V((cuts, n_f, rows, cut), BF16),
        V((groups, heads // PAIR, keys, PAIR * rows), F32),
        V((keys, PAIR * rows), F32),
        V((rows, kvw), F32),
        V((BACK, rows, kvw), BF16),
        V((BACK, rows, kvw), BF16),
        V((rows, kvw), F32),
        V((BACK, rows, kvw), BF16),
        V((BACK, rows, kvw), BF16),
        V((n_f, rows, kvw), BF16),
        V((units, cut, HEAD_SIZE), F32),
        V((units, cut, HEAD_SIZE), BF16),
        V((units, cut, HEAD_SIZE), BF16),
        strip, strip, strip, strip,
        pltpu.SMEM(doc_blocks.shape, jnp.int32),
        D((5,)), D((cuts,)),
        D((BACK, groups)), D((BACK, groups)),
        D((BACK,)), D((BACK,)), D((1,)), D((cuts, n_f)), D((cuts, n_f)),
        D((BACK, groups)), D((BACK, groups)), D((BACK, groups)), D((BACK, groups)),
        D((groups, n_f)), D((groups, n_f)), D((units,)), D((units,)),
        D((chunks,)), D((chunks,)), D((chunks,)), D((chunks,)), D((chunks,)), D((chunks,)),
    ]
    far = pl.BlockSpec(memory_space=pltpu.HBM)
    near = pl.BlockSpec(memory_space=pltpu.VMEM)
    out_shape = [
        jax.ShapeDtypeStruct(queries.shape, BF16),
        jax.ShapeDtypeStruct(key_states.shape, BF16),
        jax.ShapeDtypeStruct(key_states.shape, BF16),
        jax.ShapeDtypeStruct((width, kvw), BF16),
    ]
    held = [
        pltpu.with_memory_space_constraint(a, pltpu.HBM)
        for a in (doc_blocks, layer_inputs, queries, key_states, value_states, output_gradient)
    ]
    made = pl.pallas_call(
        functools.partial(kernel, n_s, n_f, groups, heads, cuts),
        out_shape=[pltpu.VMEM(o.shape, o.dtype) for o in out_shape],
        in_specs=[far] * 6,
        out_specs=[near] * 4,
        scratch_shapes=scratch,
        compiler_params=pltpu.CompilerParams(
            collective_id=0, has_side_effects=True, vmem_limit_bytes=VMEM_LIMIT
        ),
    )(*held)
    return tuple(
        pl.pallas_call(
            settle_outputs,
            out_shape=out_shape,
            in_specs=[near] * 4,
            out_specs=[far] * 4,
            scratch_shapes=[D((4,))],
            compiler_params=pltpu.CompilerParams(vmem_limit_bytes=SMALL_LIMIT),
        )(*made)
    )


def solution(mesh):
    sizes = dict(mesh.shape)
    return jax.shard_map(
        functools.partial(shards, sizes["seq"], sizes["fsdp"]),
        mesh=mesh,
        in_specs=(P("fsdp", "seq", None),) * 5 + (P("fsdp", None),),
        out_specs=(P("fsdp", "seq", None),) * 3 + (P("fsdp", None),),
        check_vma=False,
    )
```

```python
import functools
import math

import jax
import jax.numpy as jnp
from jax import lax
from jax.experimental import pallas as pl
from jax.experimental.pallas import tpu as pltpu
from jax.sharding import PartitionSpec as P

HEAD_SIZE = 128
BLOCK = 128
BACK = 2
PAIR = 2
SUBS = 2
EARLY = 2
SLACK = 5
LATER = 3
AHEAD = 1
HELD = 1
WHEN = 0
BEHIND = 4
VMEM_LIMIT = 40 * 1024 * 1024
SMALL_LIMIT = 8 * 1024 * 1024
MESH = pl.DeviceIdType.MESH
F32 = jnp.float32
BF16 = jnp.bfloat16


def matmul(a, b, ca, cb):
    return lax.dot_general(a, b, (((ca,), (cb,)), ((), ())), preferred_element_type=F32)


def kernel(
    n_s, n_f, groups, heads, cuts,
    doc_hbm, x_hbm, q_hbm, k_hbm, v_hbm, g_hbm,
    dq_out, dk_out, vg_out, wfin,
    q, g, kwin, vwin, xg, probs, bias,
    dv_own, dv_send, dv_recv, dk_own, dk_send, dk_recv, vgb,
    w_own, pair_send, pair_recv, right_send, left_recv, left_send, right_recv,
    doc_ref, loc_sem, xl_sem, k_ss, k_rs, v_ss, v_rs, vr_ss, x_ss, x_rs,
    dv_ss, dv_rs, dk_ss, dk_rs, vg_ss, vg_rs, p_ss, p_rs,
    r_ss, r_rs, l_ss, l_rs, f_ss, f_rs,
):
    s = lax.axis_index("seq")
    f = lax.axis_index("fsdp")
    rows = q.shape[0]
    width = wfin.shape[0]
    cut = width // cuts
    kvw = groups * HEAD_SIZE
    keys = (BACK + 1) * rows
    couples = groups // 2
    units = cuts * couples
    chunks = units * SUBS
    sub_rows = cut // SUBS
    core = s % 2
    z = s // 2
    depth = n_s // 2
    sibling = s + 1 - 2 * core
    even = core == 0
    last = z == depth - 1
    scale = 1.0 / math.sqrt(HEAD_SIZE)

    def remote(src, dst, ss, rs, to_s, to_f):
        return pltpu.make_async_remote_copy(
            src_ref=src, dst_ref=dst, send_sem=ss, recv_sem=rs,
            device_id={"seq": to_s, "fsdp": to_f}, device_id_type=MESH,
        )

    def x_cols(to, r):
        return pl.ds(pl.multiple_of(to * width + r * cut, 128), cut)

    local = [
        pltpu.make_async_copy(q_hbm.at[0], q, loc_sem.at[0]),
        pltpu.make_async_copy(k_hbm.at[0], kwin.at[BACK], loc_sem.at[1]),
        pltpu.make_async_copy(g_hbm.at[0], g, loc_sem.at[2]),
        pltpu.make_async_copy(v_hbm.at[0], vwin.at[BACK], loc_sem.at[3]),
    ]

    def own_x(r):
        return pltpu.make_async_copy(x_hbm.at[0, :, x_cols(f, r)], xg.at[r, f], xl_sem.at[r])

    doc_copy = pltpu.make_async_copy(doc_hbm, doc_ref, loc_sem.at[4])
    doc_copy.start()
    for copy in local + [own_x(r) for r in range(cuts)]:
        copy.start()

    barrier = pltpu.get_barrier_semaphore()
    for d in range(1, BACK + 1):
        @pl.when(s >= d)
        def _():
            pl.semaphore_signal(
                barrier, inc=1, device_id={"seq": s - d, "fsdp": f}, device_id_type=MESH
            )

        @pl.when(s + d < n_s)
        def _():
            pl.semaphore_signal(
                barrier, inc=1, device_id={"seq": s + d, "fsdp": f}, device_id_type=MESH
            )
    for j in range(1, n_f):
        pl.semaphore_signal(
            barrier, inc=1, device_id={"seq": s, "fsdp": (f + j) % n_f}, device_id_type=MESH
        )

    doc_copy.wait()

    def doc_of(block):
        end = jnp.int32(0)
        doc = jnp.int32(0)
        for i in range(doc_ref.shape[1]):
            end = end + doc_ref[0, i]
            doc = doc + jnp.where(block >= end, 1, 0)
        return doc

    mine = doc_of(s)
    for d in range(1, BACK + 1):
        seen = jnp.logical_and(doc_of(s - d) == mine, s >= d)
        level = jnp.where(seen, 0.0, -jnp.inf).astype(F32)
        bias[(BACK - d) * rows : (BACK - d + 1) * rows, :] = jnp.full(
            (rows, PAIR * rows), level, F32
        )
    key_at = lax.broadcasted_iota(jnp.int32, (rows, PAIR * rows), 0)
    query_at = lax.broadcasted_iota(jnp.int32, (rows, PAIR * rows), 1) % rows
    bias[BACK * rows :, :] = jnp.where(key_at <= query_at, 0.0, -jnp.inf).astype(F32)

    for d in range(1, BACK + 1):
        @pl.when(s < d)
        def _():
            kwin[BACK - d] = jnp.zeros((rows, kvw), BF16)
            vwin[BACK - d] = jnp.zeros((rows, kvw), BF16)

        @pl.when(s + d >= n_s)
        def _():
            dv_recv[d - 1] = jnp.zeros((rows, kvw), BF16)
            dk_recv[d - 1] = jnp.zeros((rows, kvw), BF16)

    @pl.when(z == 0)
    def _():
        left_recv[...] = jnp.zeros_like(left_recv)

    @pl.when(z == depth - 1)
    def _():
        right_recv[...] = jnp.zeros_like(right_recv)

    one = lambda c: jnp.where(c, 1, 0)
    pl.semaphore_wait(
        barrier, n_f - 1 + one(s >= 1) + one(s >= 2) + one(s + 1 < n_s) + one(s + 2 < n_s)
    )

    def group_cols(i):
        return pl.ds(pl.multiple_of(i * HEAD_SIZE, HEAD_SIZE), HEAD_SIZE)

    has_next = s + 1 < n_s
    even_two = jnp.logical_and(even, s + 2 < n_s)
    relays = jnp.logical_and(even, s >= 1)

    def k_copy(d, i):
        return remote(
            k_hbm.at[0, :, group_cols(i)], kwin.at[BACK - d, :, group_cols(i)],
            k_ss.at[d - 1, i], k_rs.at[d - 1, i], s + d, f,
        )

    def v_copy(d):
        return remote(
            v_hbm.at[0], vwin.at[BACK - d], v_ss.at[d - 1], v_rs.at[d - 1], s + d, f
        )

    def v_relay():
        return remote(vwin.at[BACK - 1], vwin.at[BACK - 2], vr_ss.at[0], v_rs.at[1], s + 1, f)

    def x_copy(r, j):
        to = (f + j) % n_f
        return remote(
            x_hbm.at[0, :, x_cols(to, r)], xg.at[r, f], x_ss.at[r, j], x_rs.at[r, j], s, to
        )

    def x_start(r):
        for j in range(1, n_f):
            x_copy(r, j).start()

    for i in range(groups):
        @pl.when(has_next)
        def _():
            k_copy(1, i).start()

        @pl.when(s + 2 < n_s)
        def _():
            k_copy(2, i).start()

    @pl.when(has_next)
    def _():
        v_copy(1).start()

    @pl.when(even_two)
    def _():
        v_copy(2).start()

    for r in range(EARLY):
        x_start(r)

    for copy in local[:3]:
        copy.wait()

    def back_copy(send, recv, ss, rs, d, i):
        return remote(
            send.at[d - 1, :, group_cols(i)], recv.at[d - 1, :, group_cols(i)],
            ss.at[d - 1, i], rs.at[d - 1, i], s - d, f,
        )

    def pair_of(ref, i, j):
        first = (i * heads + j * PAIR) * HEAD_SIZE
        return jnp.concatenate(
            [
                ref[:, pl.ds(pl.multiple_of(first + n * HEAD_SIZE, HEAD_SIZE), HEAD_SIZE)]
                for n in range(PAIR)
            ],
            axis=0,
        )

    def give_back(total, own, send, recv, ss, rs, i):
        own[:, group_cols(i)] = total[BACK * rows :]
        for d in range(1, BACK + 1):
            send[d - 1, :, group_cols(i)] = total[(BACK - d) * rows : (BACK - d + 1) * rows].astype(
                BF16
            )

            @pl.when(s >= d)
            def _():
                back_copy(send, recv, ss, rs, d, i).start()

    def first_pass(i):
        @pl.when(s >= 1)
        def _():
            k_copy(1, i).wait_recv()

        @pl.when(s >= 2)
        def _():
            k_copy(2, i).wait_recv()

        k_group = kwin[:, :, group_cols(i)].reshape(keys, HEAD_SIZE)
        total = jnp.zeros((keys, HEAD_SIZE), F32)
        for j in range(heads // PAIR):
            scores = matmul(k_group, pair_of(q, i, j), 1, 1)
            scores = scores * (scale * math.log2(math.e)) + bias[...]
            exps = jnp.exp2(scores - jnp.max(scores, axis=0, keepdims=True))
            p = exps * (1.0 / jnp.sum(exps, axis=0, keepdims=True))
            probs[i, j] = p
            total = total + matmul(p.astype(BF16), pair_of(g, i, j), 1, 0)
        give_back(total, dv_own, dv_send, dv_recv, dv_ss, dv_rs, i)

    def second_pass(i):
        k_group = kwin[:, :, group_cols(i)].reshape(keys, HEAD_SIZE)
        v_group = vwin[:, :, group_cols(i)].reshape(keys, HEAD_SIZE)
        k_turned = k_group.T
        total = jnp.zeros((keys, HEAD_SIZE), F32)
        for j in range(heads // PAIR):
            p = probs[i, j]
            d_probs = matmul(v_group, pair_of(g, i, j), 1, 1)
            deltas = jnp.sum(p * d_probs, axis=0, keepdims=True)
            d_scores = (p * (d_probs - deltas)).astype(BF16)
            total = total + matmul(d_scores, pair_of(q, i, j), 1, 0)
            turned = (matmul(k_turned, d_scores, 1, 0) * scale).T.astype(BF16)
            first = (i * heads + j * PAIR) * HEAD_SIZE
            for n in range(PAIR):
                cols = pl.ds(pl.multiple_of(first + n * HEAD_SIZE, HEAD_SIZE), HEAD_SIZE)
                dq_out[0, :, cols] = turned[n * rows : (n + 1) * rows]
        give_back(total * scale, dk_own, dk_send, dk_recv, dk_ss, dk_rs, i)

    def vg_copy(i, j):
        return remote(
            vgb.at[f, :, group_cols(i)], vgb.at[f, :, group_cols(i)], vg_ss.at[i, j], vg_rs.at[i, j],
            s, (f + j) % n_f,
        )

    def collect(own, recv, send, ss, rs, i):
        for d in range(1, BACK + 1):
            @pl.when(s + d < n_s)
            def _():
                back_copy(send, recv, ss, rs, d, i).wait_recv()
        cols = group_cols(i)
        total = own[:, cols]
        for d in range(1, BACK + 1):
            total = total + recv[d - 1, :, cols].astype(F32)
        return total.astype(BF16)

    def value(i):
        done = collect(dv_own, dv_recv, dv_send, dv_ss, dv_rs, i)
        vgb[f, :, group_cols(i)] = done
        vg_out[0, :, group_cols(i)] = done
        for j in range(1, n_f):
            vg_copy(i, j).start()

    def place_of(u):
        early = u < 2 * couples
        return jnp.where(early, u % 2, u // couples), jnp.where(early, u // 2, u % couples)

    def pair_copy(u):
        return remote(pair_send.at[u], pair_recv.at[u], p_ss.at[u], p_rs.at[u], sibling, f)

    def weight_unit(u):
        r, p = place_of(jnp.int32(u))

        @pl.when(r == 0)
        def _():
            for n in range(2):
                for j in range(1, n_f):
                    vg_copy(2 * p + n, j).wait_recv()

        @pl.when(p == 0)
        def _():
            own_x(r).wait()
            for j in range(1, n_f):
                x_copy(r, j).wait_recv()

        cols = pl.ds(pl.multiple_of(2 * p * HEAD_SIZE, 2 * HEAD_SIZE), 2 * HEAD_SIZE)
        values = vgb[:, :, cols].reshape(n_f * rows, 2 * HEAD_SIZE)
        part = matmul(xg[r].reshape(n_f * rows, cut), values, 0, 0)
        first, second = part[:, :HEAD_SIZE], part[:, HEAD_SIZE:]
        w_own[u] = jnp.where(even, first, second)
        pair_send[u] = jnp.where(even, second, first).astype(BF16)
        pair_copy(u).start()

    def right_copy(c):
        return remote(right_send.at[c], left_recv.at[c], r_ss.at[c], r_rs.at[c], s + 2, f)

    def left_copy(c):
        return remote(left_send.at[c], right_recv.at[c], l_ss.at[c], l_rs.at[c], s - 2, f)

    def place(c, side):
        r, p = place_of(c // SUBS)
        at = r * cut + (c % SUBS) * sub_rows
        return wfin.at[
            pl.ds(pl.multiple_of(at, sub_rows), sub_rows), group_cols(2 * p + side)
        ]

    def final_copy(c):
        return remote(place(c, core), place(c, core), f_ss.at[c], f_rs.at[c], sibling, f)

    def own_chunk(c):
        return w_own[c // SUBS, pl.ds(pl.multiple_of((c % SUBS) * sub_rows, sub_rows), sub_rows), :]

    token_count = n_f * n_s * rows

    def step(t, carry):
        to_right = t - SLACK * z - LATER
        to_left = t - SLACK * (depth - 1 - z)
        done = jnp.minimum(to_right, to_left)

        def inside(c):
            return jnp.logical_and(c >= 0, c < chunks)

        @pl.when(jnp.logical_and(inside(to_left), z < depth - 1))
        def _():
            left_copy(to_left).wait_recv()

        @pl.when(jnp.logical_and(inside(to_left), z > 0))
        def _():
            left_send[to_left] = (own_chunk(to_left) + right_recv[to_left].astype(F32)).astype(BF16)
            left_copy(to_left).start()

        @pl.when(jnp.logical_and(inside(to_right), z > 0))
        def _():
            right_copy(to_right).wait_recv()

        @pl.when(jnp.logical_and(inside(to_right), z < depth - 1))
        def _():
            right_send[to_right] = (own_chunk(to_right) + left_recv[to_right].astype(F32)).astype(
                BF16
            )
            right_copy(to_right).start()

        @pl.when(inside(done))
        def _():
            total = own_chunk(done) + left_recv[done].astype(F32) + right_recv[done].astype(F32)
            place(done, core)[...] = (total * (1.0 / math.sqrt(token_count))).astype(BF16)
            final_copy(done).start()

        return carry

    lag = jnp.where(last, 1, 3)
    ready = groups - lag

    def first_loop(i, carry):
        @pl.when(jnp.logical_and(i >= lag, jnp.logical_not(last)))
        def _():
            value(i - lag)

        first_pass(i)

        @pl.when(jnp.logical_and(i >= lag, last))
        def _():
            value(i - lag)

        return carry

    lax.fori_loop(0, groups, first_loop, 0)

    local[3].wait()
    @pl.when(s >= 1)
    def _():
        v_copy(1).wait_recv()

    @pl.when(relays)
    def _():
        v_relay().start()

    @pl.when(s >= 2)
    def _():
        v_copy(2).wait_recv()

    early = jnp.where(last, 0, jnp.where(z == depth - 2, groups - HELD, groups))

    def value_loop(k, carry):
        @pl.when(k < groups - 1)
        def _():
            value(k)

        @pl.when(jnp.logical_and(k >= 1, k <= early))
        def _():
            second_pass(k - 1)

        @pl.when(k == groups - 1)
        def _():
            value(k)
            for r in range(EARLY, cuts):
                x_start(r)

        return carry

    lax.fori_loop(ready, groups, value_loop, 0)

    def settle(c, carry):
        other = remote(place(c, 1 - core), place(c, 1 - core), f_ss.at[c], f_rs.at[c], sibling, f)
        other.wait_recv()
        final_copy(c).wait_send()

        @pl.when(z < depth - 1)
        def _():
            right_copy(c).wait_send()

        @pl.when(z > 0)
        def _():
            left_copy(c).wait_send()

        return carry

    def tidy():
        for i in range(groups):
            dk_out[0, :, i * HEAD_SIZE : (i + 1) * HEAD_SIZE] = collect(
                dk_own, dk_recv, dk_send, dk_ss, dk_rs, i
            )

        @pl.when(has_next)
        def _():
            v_copy(1).wait_send()
            for i in range(groups):
                k_copy(1, i).wait_send()

        @pl.when(s + 2 < n_s)
        def _():
            for i in range(groups):
                k_copy(2, i).wait_send()

        @pl.when(even_two)
        def _():
            v_copy(2).wait_send()

        @pl.when(relays)
        def _():
            v_relay().wait_send()

        for d in range(1, BACK + 1):
            @pl.when(s >= d)
            def _():
                for i in range(groups):
                    back_copy(dv_send, dv_recv, dv_ss, dv_rs, d, i).wait_send()
                    back_copy(dk_send, dk_recv, dk_ss, dk_rs, d, i).wait_send()
        for j in range(1, n_f):
            for r in range(cuts):
                x_copy(r, j).wait_send()
            for i in range(groups):
                vg_copy(i, j).wait_send()
        for u in range(units):
            pair_copy(u).wait_send()

    shift = jnp.minimum(SLACK * (depth - 1 - z), SLACK * z + LATER)

    def second_loop(i, carry):
        second_pass(i)
        return carry

    total = chunks + SLACK * (depth - 1) + LATER

    def line(t, carry):
        own = t - shift
        u = own // SUBS

        @pl.when(jnp.logical_and(own % SUBS == 0, jnp.logical_and(own >= 0, u + AHEAD < units)))
        def _():
            weight_unit(u + AHEAD)

        @pl.when(jnp.logical_and(own % SUBS == 0, jnp.logical_and(own >= 0, u < units)))
        def _():
            pair_copy(u).wait_recv()
            w_own[u] = w_own[u] + pair_recv[u].astype(F32)

        step(t, carry)
        behind = jnp.minimum(t - SLACK * z - LATER, t - SLACK * (depth - 1 - z)) - BEHIND

        @pl.when(jnp.logical_and(behind >= 0, behind < chunks - BEHIND))
        def _():
            settle(behind, 0)

        @pl.when(t == total - BEHIND)
        def _():
            tidy()

        @pl.when(own == chunks - 1 - jnp.where(last, 0, WHEN))
        def _():
            lax.fori_loop(early, groups, second_loop, 0)

        return carry

    for u in range(AHEAD):
        weight_unit(u)
    lax.fori_loop(jnp.where(z < depth - 2, groups - 1, groups), groups, second_loop, 0)
    lax.fori_loop(0, total, line, 0)

    lax.fori_loop(chunks - BEHIND, chunks, settle, 0)


def settle_outputs(*refs):
    sources, outs, sems = refs[:4], refs[4:8], refs[8]
    saves = [pltpu.make_async_copy(sources[i], outs[i], sems.at[i]) for i in range(4)]
    for save in saves:
        save.start()
    for save in saves:
        save.wait()


def shards(n_s, n_f, layer_inputs, queries, key_states, value_states, output_gradient, doc_blocks):
    rows = queries.shape[1]
    kvw = key_states.shape[2]
    groups = kvw // HEAD_SIZE
    heads = queries.shape[2] // kvw
    width = layer_inputs.shape[2] // n_f
    cuts = 4 if width % (4 * 128) == 0 else 2
    cut = width // cuts
    units = cuts * (groups // 2)
    chunks = units * SUBS
    keys = (BACK + 1) * rows
    V = pltpu.VMEM
    D = pltpu.SemaphoreType.DMA
    strip = V((chunks, cut // SUBS, HEAD_SIZE), BF16)
    scratch = [
        V((rows, queries.shape[2]), BF16),
        V((rows, queries.shape[2]), BF16),
        V((BACK + 1, rows, kvw), BF16),
        V((BACK + 1, rows, kvw), BF16),
        V((cuts, n_f, rows, cut), BF16),
        V((groups, heads // PAIR, keys, PAIR * rows), F32),
        V((keys, PAIR * rows), F32),
        V((rows, kvw), F32),
        V((BACK, rows, kvw), BF16),
        V((BACK, rows, kvw), BF16),
        V((rows, kvw), F32),
        V((BACK, rows, kvw), BF16),
        V((BACK, rows, kvw), BF16),
        V((n_f, rows, kvw), BF16),
        V((units, cut, HEAD_SIZE), F32),
        V((units, cut, HEAD_SIZE), BF16),
        V((units, cut, HEAD_SIZE), BF16),
        strip, strip, strip, strip,
        pltpu.SMEM(doc_blocks.shape, jnp.int32),
        D((5,)), D((cuts,)),
        D((BACK, groups)), D((BACK, groups)),
        D((BACK,)), D((BACK,)), D((1,)), D((cuts, n_f)), D((cuts, n_f)),
        D((BACK, groups)), D((BACK, groups)), D((BACK, groups)), D((BACK, groups)),
        D((groups, n_f)), D((groups, n_f)), D((units,)), D((units,)),
        D((chunks,)), D((chunks,)), D((chunks,)), D((chunks,)), D((chunks,)), D((chunks,)),
    ]
    far = pl.BlockSpec(memory_space=pltpu.HBM)
    near = pl.BlockSpec(memory_space=pltpu.VMEM)
    out_shape = [
        jax.ShapeDtypeStruct(queries.shape, BF16),
        jax.ShapeDtypeStruct(key_states.shape, BF16),
        jax.ShapeDtypeStruct(key_states.shape, BF16),
        jax.ShapeDtypeStruct((width, kvw), BF16),
    ]
    held = [
        pltpu.with_memory_space_constraint(a, pltpu.HBM)
        for a in (doc_blocks, layer_inputs, queries, key_states, value_states, output_gradient)
    ]
    made = pl.pallas_call(
        functools.partial(kernel, n_s, n_f, groups, heads, cuts),
        out_shape=[pltpu.VMEM(o.shape, o.dtype) for o in out_shape],
        in_specs=[far] * 6,
        out_specs=[near] * 4,
        scratch_shapes=scratch,
        compiler_params=pltpu.CompilerParams(
            collective_id=0, has_side_effects=True, vmem_limit_bytes=VMEM_LIMIT
        ),
    )(*held)
    return tuple(
        pl.pallas_call(
            settle_outputs,
            out_shape=out_shape,
            in_specs=[near] * 4,
            out_specs=[far] * 4,
            scratch_shapes=[D((4,))],
            compiler_params=pltpu.CompilerParams(vmem_limit_bytes=SMALL_LIMIT),
        )(*made)
    )


def solution(mesh):
    sizes = dict(mesh.shape)
    return jax.shard_map(
        functools.partial(shards, sizes["seq"], sizes["fsdp"]),
        mesh=mesh,
        in_specs=(P("fsdp", "seq", None),) * 5 + (P("fsdp", None),),
        out_specs=(P("fsdp", "seq", None),) * 3 + (P("fsdp", None),),
        check_vma=False,
    )
```

```python
import functools
import math

import jax
import jax.numpy as jnp
from jax import lax
from jax.experimental import pallas as pl
from jax.experimental.pallas import tpu as pltpu
from jax.sharding import PartitionSpec as P

HEAD_SIZE = 128
BLOCK = 128
BACK = 2
PAIR = 2
SUBS = 2
EARLY = 2
SLACK = 5
LATER = 4
AHEAD = 1
HELD = 2
FROM = 5
EVERY = 2
BEHIND = 4
VMEM_LIMIT = 40 * 1024 * 1024
SMALL_LIMIT = 8 * 1024 * 1024
MESH = pl.DeviceIdType.MESH
F32 = jnp.float32
BF16 = jnp.bfloat16


def matmul(a, b, ca, cb):
    return lax.dot_general(a, b, (((ca,), (cb,)), ((), ())), preferred_element_type=F32)


def kernel(
    n_s, n_f, groups, heads, cuts,
    doc_hbm, x_hbm, q_hbm, k_hbm, v_hbm, g_hbm,
    dq_out, dk_out, vg_out, wfin,
    q, g, kwin, vwin, xg, probs, bias,
    dv_own, dv_send, dv_recv, dk_own, dk_send, dk_recv, vgb,
    w_own, pair_send, pair_recv, right_send, left_recv, left_send, right_recv,
    doc_ref, loc_sem, xl_sem, k_ss, k_rs, v_ss, v_rs, vr_ss, x_ss, x_rs,
    dv_ss, dv_rs, dk_ss, dk_rs, vg_ss, vg_rs, p_ss, p_rs,
    r_ss, r_rs, l_ss, l_rs, f_ss, f_rs, held,
):
    s = lax.axis_index("seq")
    f = lax.axis_index("fsdp")
    rows = q.shape[0]
    width = wfin.shape[0]
    cut = width // cuts
    kvw = groups * HEAD_SIZE
    keys = (BACK + 1) * rows
    couples = groups // 2
    units = cuts * couples
    chunks = units * SUBS
    sub_rows = cut // SUBS
    core = s % 2
    z = s // 2
    depth = n_s // 2
    sibling = s + 1 - 2 * core
    even = core == 0
    last = z == depth - 1
    scale = 1.0 / math.sqrt(HEAD_SIZE)

    def remote(src, dst, ss, rs, to_s, to_f):
        return pltpu.make_async_remote_copy(
            src_ref=src, dst_ref=dst, send_sem=ss, recv_sem=rs,
            device_id={"seq": to_s, "fsdp": to_f}, device_id_type=MESH,
        )

    def x_cols(to, r):
        return pl.ds(pl.multiple_of(to * width + r * cut, 128), cut)

    local = [
        pltpu.make_async_copy(q_hbm.at[0], q, loc_sem.at[0]),
        pltpu.make_async_copy(k_hbm.at[0], kwin.at[BACK], loc_sem.at[1]),
        pltpu.make_async_copy(g_hbm.at[0], g, loc_sem.at[2]),
        pltpu.make_async_copy(v_hbm.at[0], vwin.at[BACK], loc_sem.at[3]),
    ]

    def own_x(r):
        return pltpu.make_async_copy(x_hbm.at[0, :, x_cols(f, r)], xg.at[r, f], xl_sem.at[r])

    doc_copy = pltpu.make_async_copy(doc_hbm, doc_ref, loc_sem.at[4])
    doc_copy.start()
    for copy in local + [own_x(r) for r in range(cuts)]:
        copy.start()

    barrier = pltpu.get_barrier_semaphore()
    for d in range(1, BACK + 1):
        @pl.when(s >= d)
        def _():
            pl.semaphore_signal(
                barrier, inc=1, device_id={"seq": s - d, "fsdp": f}, device_id_type=MESH
            )

        @pl.when(s + d < n_s)
        def _():
            pl.semaphore_signal(
                barrier, inc=1, device_id={"seq": s + d, "fsdp": f}, device_id_type=MESH
            )
    for j in range(1, n_f):
        pl.semaphore_signal(
            barrier, inc=1, device_id={"seq": s, "fsdp": (f + j) % n_f}, device_id_type=MESH
        )

    doc_copy.wait()

    def doc_of(block):
        end = jnp.int32(0)
        doc = jnp.int32(0)
        for i in range(doc_ref.shape[1]):
            end = end + doc_ref[0, i]
            doc = doc + jnp.where(block >= end, 1, 0)
        return doc

    mine = doc_of(s)
    for d in range(1, BACK + 1):
        seen = jnp.logical_and(doc_of(s - d) == mine, s >= d)
        level = jnp.where(seen, 0.0, -jnp.inf).astype(F32)
        bias[(BACK - d) * rows : (BACK - d + 1) * rows, :] = jnp.full(
            (rows, PAIR * rows), level, F32
        )
    key_at = lax.broadcasted_iota(jnp.int32, (rows, PAIR * rows), 0)
    query_at = lax.broadcasted_iota(jnp.int32, (rows, PAIR * rows), 1) % rows
    bias[BACK * rows :, :] = jnp.where(key_at <= query_at, 0.0, -jnp.inf).astype(F32)

    for d in range(1, BACK + 1):
        @pl.when(s < d)
        def _():
            kwin[BACK - d] = jnp.zeros((rows, kvw), BF16)
            vwin[BACK - d] = jnp.zeros((rows, kvw), BF16)

        @pl.when(s + d >= n_s)
        def _():
            dv_recv[d - 1] = jnp.zeros((rows, kvw), BF16)
            dk_recv[d - 1] = jnp.zeros((rows, kvw), BF16)

    @pl.when(z == 0)
    def _():
        left_recv[...] = jnp.zeros_like(left_recv)

    @pl.when(z == depth - 1)
    def _():
        right_recv[...] = jnp.zeros_like(right_recv)

    one = lambda c: jnp.where(c, 1, 0)
    pl.semaphore_wait(
        barrier, n_f - 1 + one(s >= 1) + one(s >= 2) + one(s + 1 < n_s) + one(s + 2 < n_s)
    )

    def group_cols(i):
        return pl.ds(pl.multiple_of(i * HEAD_SIZE, HEAD_SIZE), HEAD_SIZE)

    has_next = s + 1 < n_s
    even_two = jnp.logical_and(even, s + 2 < n_s)
    relays = jnp.logical_and(even, s >= 1)

    def k_copy(d, i):
        return remote(
            k_hbm.at[0, :, group_cols(i)], kwin.at[BACK - d, :, group_cols(i)],
            k_ss.at[d - 1, i], k_rs.at[d - 1, i], s + d, f,
        )

    def v_copy(d):
        return remote(
            v_hbm.at[0], vwin.at[BACK - d], v_ss.at[d - 1], v_rs.at[d - 1], s + d, f
        )

    def v_relay():
        return remote(vwin.at[BACK - 1], vwin.at[BACK - 2], vr_ss.at[0], v_rs.at[1], s + 1, f)

    def x_copy(r, j):
        to = (f + j) % n_f
        return remote(
            x_hbm.at[0, :, x_cols(to, r)], xg.at[r, f], x_ss.at[r, j], x_rs.at[r, j], s, to
        )

    def x_start(r):
        for j in range(1, n_f):
            x_copy(r, j).start()

    for i in range(groups):
        @pl.when(has_next)
        def _():
            k_copy(1, i).start()

        @pl.when(s + 2 < n_s)
        def _():
            k_copy(2, i).start()

    @pl.when(has_next)
    def _():
        v_copy(1).start()

    @pl.when(even_two)
    def _():
        v_copy(2).start()

    for r in range(EARLY):
        x_start(r)

    for copy in local[:3]:
        copy.wait()

    def back_copy(send, recv, ss, rs, d, i):
        return remote(
            send.at[d - 1, :, group_cols(i)], recv.at[d - 1, :, group_cols(i)],
            ss.at[d - 1, i], rs.at[d - 1, i], s - d, f,
        )

    def pair_of(ref, i, j):
        first = (i * heads + j * PAIR) * HEAD_SIZE
        return jnp.concatenate(
            [
                ref[:, pl.ds(pl.multiple_of(first + n * HEAD_SIZE, HEAD_SIZE), HEAD_SIZE)]
                for n in range(PAIR)
            ],
            axis=0,
        )

    def give_back(total, own, send, recv, ss, rs, i):
        own[:, group_cols(i)] = total[BACK * rows :]
        for d in range(1, BACK + 1):
            send[d - 1, :, group_cols(i)] = total[(BACK - d) * rows : (BACK - d + 1) * rows].astype(
                BF16
            )

            @pl.when(s >= d)
            def _():
                back_copy(send, recv, ss, rs, d, i).start()

    def first_pass(i):
        @pl.when(s >= 1)
        def _():
            k_copy(1, i).wait_recv()

        @pl.when(s >= 2)
        def _():
            k_copy(2, i).wait_recv()

        k_group = kwin[:, :, group_cols(i)].reshape(keys, HEAD_SIZE)
        total = jnp.zeros((keys, HEAD_SIZE), F32)
        for j in range(heads // PAIR):
            scores = matmul(k_group, pair_of(q, i, j), 1, 1)
            scores = scores * (scale * math.log2(math.e)) + bias[...]
            exps = jnp.exp2(scores - jnp.max(scores, axis=0, keepdims=True))
            p = exps * (1.0 / jnp.sum(exps, axis=0, keepdims=True))
            probs[i, j] = p
            total = total + matmul(p.astype(BF16), pair_of(g, i, j), 1, 0)
        give_back(total, dv_own, dv_send, dv_recv, dv_ss, dv_rs, i)

    def second_part(i, j, k_group, v_group, k_turned):
        p = probs[i, j]
        d_probs = matmul(v_group, pair_of(g, i, j), 1, 1)
        deltas = jnp.sum(p * d_probs, axis=0, keepdims=True)
        d_scores = (p * (d_probs - deltas)).astype(BF16)
        turned = (matmul(k_turned, d_scores, 1, 0) * scale).T.astype(BF16)
        first = (i * heads + j * PAIR) * HEAD_SIZE
        for n in range(PAIR):
            cols = pl.ds(pl.multiple_of(first + n * HEAD_SIZE, HEAD_SIZE), HEAD_SIZE)
            dq_out[0, :, cols] = turned[n * rows : (n + 1) * rows]
        return matmul(d_scores, pair_of(q, i, j), 1, 0)

    def second_pass(i):
        k_group = kwin[:, :, group_cols(i)].reshape(keys, HEAD_SIZE)
        v_group = vwin[:, :, group_cols(i)].reshape(keys, HEAD_SIZE)
        k_turned = k_group.T
        total = jnp.zeros((keys, HEAD_SIZE), F32)
        for j in range(heads // PAIR):
            total = total + second_part(i, j, k_group, v_group, k_turned)
        give_back(total * scale, dk_own, dk_send, dk_recv, dk_ss, dk_rs, i)

    def second_piece(i, j):
        @pl.when(j == 0)
        def _():
            held[...] = jnp.zeros_like(held)

        k_group = kwin[:, :, group_cols(i)].reshape(keys, HEAD_SIZE)
        v_group = vwin[:, :, group_cols(i)].reshape(keys, HEAD_SIZE)
        held[...] = held[...] + second_part(i, j, k_group, v_group, k_group.T)

        @pl.when(j == heads // PAIR - 1)
        def _():
            give_back(held[...] * scale, dk_own, dk_send, dk_recv, dk_ss, dk_rs, i)

    def vg_copy(i, j):
        return remote(
            vgb.at[f, :, group_cols(i)], vgb.at[f, :, group_cols(i)], vg_ss.at[i, j], vg_rs.at[i, j],
            s, (f + j) % n_f,
        )

    def collect(own, recv, send, ss, rs, i):
        for d in range(1, BACK + 1):
            @pl.when(s + d < n_s)
            def _():
                back_copy(send, recv, ss, rs, d, i).wait_recv()
        cols = group_cols(i)
        total = own[:, cols]
        for d in range(1, BACK + 1):
            total = total + recv[d - 1, :, cols].astype(F32)
        return total.astype(BF16)

    def value(i):
        done = collect(dv_own, dv_recv, dv_send, dv_ss, dv_rs, i)
        vgb[f, :, group_cols(i)] = done
        vg_out[0, :, group_cols(i)] = done
        for j in range(1, n_f):
            vg_copy(i, j).start()

    def place_of(u):
        early = u < 2 * couples
        return jnp.where(early, u % 2, u // couples), jnp.where(early, u // 2, u % couples)

    def pair_copy(u):
        return remote(pair_send.at[u], pair_recv.at[u], p_ss.at[u], p_rs.at[u], sibling, f)

    def weight_unit(u):
        r, p = place_of(jnp.int32(u))

        @pl.when(r == 0)
        def _():
            for n in range(2):
                for j in range(1, n_f):
                    vg_copy(2 * p + n, j).wait_recv()

        @pl.when(p == 0)
        def _():
            own_x(r).wait()
            for j in range(1, n_f):
                x_copy(r, j).wait_recv()

        cols = pl.ds(pl.multiple_of(2 * p * HEAD_SIZE, 2 * HEAD_SIZE), 2 * HEAD_SIZE)
        values = vgb[:, :, cols].reshape(n_f * rows, 2 * HEAD_SIZE)
        part = matmul(xg[r].reshape(n_f * rows, cut), values, 0, 0)
        first, second = part[:, :HEAD_SIZE], part[:, HEAD_SIZE:]
        w_own[u] = jnp.where(even, first, second)
        pair_send[u] = jnp.where(even, second, first).astype(BF16)
        pair_copy(u).start()

    def right_copy(c):
        return remote(right_send.at[c], left_recv.at[c], r_ss.at[c], r_rs.at[c], s + 2, f)

    def left_copy(c):
        return remote(left_send.at[c], right_recv.at[c], l_ss.at[c], l_rs.at[c], s - 2, f)

    def place(c, side):
        r, p = place_of(c // SUBS)
        at = r * cut + (c % SUBS) * sub_rows
        return wfin.at[
            pl.ds(pl.multiple_of(at, sub_rows), sub_rows), group_cols(2 * p + side)
        ]

    def final_copy(c):
        return remote(place(c, core), place(c, core), f_ss.at[c], f_rs.at[c], sibling, f)

    def own_chunk(c):
        return w_own[c // SUBS, pl.ds(pl.multiple_of((c % SUBS) * sub_rows, sub_rows), sub_rows), :]

    token_count = n_f * n_s * rows

    def step(t, carry):
        to_right = t - SLACK * z - LATER
        to_left = t - SLACK * (depth - 1 - z)
        done = jnp.minimum(to_right, to_left)

        def inside(c):
            return jnp.logical_and(c >= 0, c < chunks)

        @pl.when(jnp.logical_and(inside(to_left), z < depth - 1))
        def _():
            left_copy(to_left).wait_recv()

        @pl.when(jnp.logical_and(inside(to_left), z > 0))
        def _():
            left_send[to_left] = (own_chunk(to_left) + right_recv[to_left].astype(F32)).astype(BF16)
            left_copy(to_left).start()

        @pl.when(jnp.logical_and(inside(to_right), z > 0))
        def _():
            right_copy(to_right).wait_recv()

        @pl.when(jnp.logical_and(inside(to_right), z < depth - 1))
        def _():
            right_send[to_right] = (own_chunk(to_right) + left_recv[to_right].astype(F32)).astype(
                BF16
            )
            right_copy(to_right).start()

        @pl.when(inside(done))
        def _():
            total = own_chunk(done) + left_recv[done].astype(F32) + right_recv[done].astype(F32)
            place(done, core)[...] = (total * (1.0 / math.sqrt(token_count))).astype(BF16)
            final_copy(done).start()

        return carry

    lag = jnp.where(last, 1, 3)
    ready = groups - lag

    def first_loop(i, carry):
        @pl.when(jnp.logical_and(i >= lag, jnp.logical_not(last)))
        def _():
            value(i - lag)

        first_pass(i)

        @pl.when(jnp.logical_and(i >= lag, last))
        def _():
            value(i - lag)

        return carry

    lax.fori_loop(0, groups, first_loop, 0)

    local[3].wait()
    @pl.when(s >= 1)
    def _():
        v_copy(1).wait_recv()

    @pl.when(relays)
    def _():
        v_relay().start()

    @pl.when(s >= 2)
    def _():
        v_copy(2).wait_recv()

    early = jnp.where(last, 0, jnp.where(z == depth - 2, groups - HELD, groups))

    def value_loop(k, carry):
        @pl.when(k < groups - 1)
        def _():
            value(k)

        @pl.when(jnp.logical_and(k >= 1, k <= early))
        def _():
            second_pass(k - 1)

        @pl.when(k == groups - 1)
        def _():
            value(k)
            for r in range(EARLY, cuts):
                x_start(r)

        return carry

    lax.fori_loop(ready, groups, value_loop, 0)

    def settle(c, carry):
        other = remote(place(c, 1 - core), place(c, 1 - core), f_ss.at[c], f_rs.at[c], sibling, f)
        other.wait_recv()
        final_copy(c).wait_send()

        @pl.when(z < depth - 1)
        def _():
            right_copy(c).wait_send()

        @pl.when(z > 0)
        def _():
            left_copy(c).wait_send()

        return carry

    def tidy():
        for i in range(groups):
            dk_out[0, :, i * HEAD_SIZE : (i + 1) * HEAD_SIZE] = collect(
                dk_own, dk_recv, dk_send, dk_ss, dk_rs, i
            )

        @pl.when(has_next)
        def _():
            v_copy(1).wait_send()
            for i in range(groups):
                k_copy(1, i).wait_send()

        @pl.when(s + 2 < n_s)
        def _():
            for i in range(groups):
                k_copy(2, i).wait_send()

        @pl.when(even_two)
        def _():
            v_copy(2).wait_send()

        @pl.when(relays)
        def _():
            v_relay().wait_send()

        for d in range(1, BACK + 1):
            @pl.when(s >= d)
            def _():
                for i in range(groups):
                    back_copy(dv_send, dv_recv, dv_ss, dv_rs, d, i).wait_send()
                    back_copy(dk_send, dk_recv, dk_ss, dk_rs, d, i).wait_send()
        for j in range(1, n_f):
            for r in range(cuts):
                x_copy(r, j).wait_send()
            for i in range(groups):
                vg_copy(i, j).wait_send()
        for u in range(units):
            pair_copy(u).wait_send()

    shift = jnp.minimum(SLACK * (depth - 1 - z), SLACK * z + LATER)

    def second_loop(i, carry):
        second_pass(i)
        return carry

    total = chunks + SLACK * (depth - 1) + LATER
    parts = heads // PAIR

    def line(t, carry):
        own = t - shift
        u = own // SUBS

        @pl.when(jnp.logical_and(own % SUBS == 0, jnp.logical_and(own >= 0, u + AHEAD < units)))
        def _():
            weight_unit(u + AHEAD)

        @pl.when(jnp.logical_and(own % SUBS == 0, jnp.logical_and(own >= 0, u < units)))
        def _():
            pair_copy(u).wait_recv()
            w_own[u] = w_own[u] + pair_recv[u].astype(F32)

        step(t, carry)
        behind = jnp.minimum(t - SLACK * z - LATER, t - SLACK * (depth - 1 - z)) - BEHIND

        @pl.when(jnp.logical_and(behind >= 0, behind < chunks - BEHIND))
        def _():
            settle(behind, 0)

        @pl.when(t == total - BEHIND)
        def _():
            tidy()

        @pl.when(jnp.logical_and(own == chunks - 1, last))
        def _():
            lax.fori_loop(early, groups, second_loop, 0)

        piece = (own - FROM) // EVERY
        turn = jnp.logical_and(own >= FROM, (own - FROM) % EVERY == 0)

        @pl.when(jnp.logical_and(jnp.logical_and(turn, z == depth - 2), piece < HELD * parts))
        def _():
            second_piece(groups - HELD + piece // parts, piece % parts)

        return carry

    for u in range(AHEAD):
        weight_unit(u)
    lax.fori_loop(jnp.where(z < depth - 2, groups - 1, groups), groups, second_loop, 0)
    lax.fori_loop(0, total, line, 0)

    lax.fori_loop(chunks - BEHIND, chunks, settle, 0)


def settle_outputs(*refs):
    sources, outs, sems = refs[:4], refs[4:8], refs[8]
    saves = [pltpu.make_async_copy(sources[i], outs[i], sems.at[i]) for i in range(4)]
    for save in saves:
        save.start()
    for save in saves:
        save.wait()


def shards(n_s, n_f, layer_inputs, queries, key_states, value_states, output_gradient, doc_blocks):
    rows = queries.shape[1]
    kvw = key_states.shape[2]
    groups = kvw // HEAD_SIZE
    heads = queries.shape[2] // kvw
    width = layer_inputs.shape[2] // n_f
    cuts = 4 if width % (4 * 128) == 0 else 2
    cut = width // cuts
    units = cuts * (groups // 2)
    chunks = units * SUBS
    keys = (BACK + 1) * rows
    V = pltpu.VMEM
    D = pltpu.SemaphoreType.DMA
    strip = V((chunks, cut // SUBS, HEAD_SIZE), BF16)
    scratch = [
        V((rows, queries.shape[2]), BF16),
        V((rows, queries.shape[2]), BF16),
        V((BACK + 1, rows, kvw), BF16),
        V((BACK + 1, rows, kvw), BF16),
        V((cuts, n_f, rows, cut), BF16),
        V((groups, heads // PAIR, keys, PAIR * rows), F32),
        V((keys, PAIR * rows), F32),
        V((rows, kvw), F32),
        V((BACK, rows, kvw), BF16),
        V((BACK, rows, kvw), BF16),
        V((rows, kvw), F32),
        V((BACK, rows, kvw), BF16),
        V((BACK, rows, kvw), BF16),
        V((n_f, rows, kvw), BF16),
        V((units, cut, HEAD_SIZE), F32),
        V((units, cut, HEAD_SIZE), BF16),
        V((units, cut, HEAD_SIZE), BF16),
        strip, strip, strip, strip,
        pltpu.SMEM(doc_blocks.shape, jnp.int32),
        D((5,)), D((cuts,)),
        D((BACK, groups)), D((BACK, groups)),
        D((BACK,)), D((BACK,)), D((1,)), D((cuts, n_f)), D((cuts, n_f)),
        D((BACK, groups)), D((BACK, groups)), D((BACK, groups)), D((BACK, groups)),
        D((groups, n_f)), D((groups, n_f)), D((units,)), D((units,)),
        D((chunks,)), D((chunks,)), D((chunks,)), D((chunks,)), D((chunks,)), D((chunks,)),
        V((keys, HEAD_SIZE), F32),
    ]
    far = pl.BlockSpec(memory_space=pltpu.HBM)
    near = pl.BlockSpec(memory_space=pltpu.VMEM)
    out_shape = [
        jax.ShapeDtypeStruct(queries.shape, BF16),
        jax.ShapeDtypeStruct(key_states.shape, BF16),
        jax.ShapeDtypeStruct(key_states.shape, BF16),
        jax.ShapeDtypeStruct((width, kvw), BF16),
    ]
    held = [
        pltpu.with_memory_space_constraint(a, pltpu.HBM)
        for a in (doc_blocks, layer_inputs, queries, key_states, value_states, output_gradient)
    ]
    made = pl.pallas_call(
        functools.partial(kernel, n_s, n_f, groups, heads, cuts),
        out_shape=[pltpu.VMEM(o.shape, o.dtype) for o in out_shape],
        in_specs=[far] * 6,
        out_specs=[near] * 4,
        scratch_shapes=scratch,
        compiler_params=pltpu.CompilerParams(
            collective_id=0, has_side_effects=True, vmem_limit_bytes=VMEM_LIMIT
        ),
    )(*held)
    return tuple(
        pl.pallas_call(
            settle_outputs,
            out_shape=out_shape,
            in_specs=[near] * 4,
            out_specs=[far] * 4,
            scratch_shapes=[D((4,))],
            compiler_params=pltpu.CompilerParams(vmem_limit_bytes=SMALL_LIMIT),
        )(*made)
    )


def solution(mesh):
    sizes = dict(mesh.shape)
    return jax.shard_map(
        functools.partial(shards, sizes["seq"], sizes["fsdp"]),
        mesh=mesh,
        in_specs=(P("fsdp", "seq", None),) * 5 + (P("fsdp", None),),
        out_specs=(P("fsdp", "seq", None),) * 3 + (P("fsdp", None),),
        check_vma=False,
    )
```

```python
import functools
import math

import jax
import jax.numpy as jnp
from jax import lax
from jax.experimental import pallas as pl
from jax.experimental.pallas import tpu as pltpu
from jax.sharding import PartitionSpec as P

HEAD_SIZE = 128
BLOCK = 128
BACK = 2
PAIR = 2
SUBS = 2
EARLY = 2
SLACK = 5
LATER = 4
AHEAD = 1
HELD = 2
FROM = 5
EVERY = 2
BEHIND = 4
VMEM_LIMIT = 40 * 1024 * 1024
SMALL_LIMIT = 8 * 1024 * 1024
MESH = pl.DeviceIdType.MESH
F32 = jnp.float32
BF16 = jnp.bfloat16


def matmul(a, b, ca, cb):
    return lax.dot_general(a, b, (((ca,), (cb,)), ((), ())), preferred_element_type=F32)


def kernel(
    n_s, n_f, groups, heads, cuts,
    doc_hbm, x_hbm, q_hbm, k_hbm, v_hbm, g_hbm,
    dq_out, dk_out, vg_out, wfin,
    q, g, kwin, vwin, xg, probs, bias,
    dv_own, dv_send, dv_recv, dk_own, dk_send, dk_recv, vgb,
    w_own, pair_send, pair_recv, right_send, left_recv, left_send, right_recv,
    doc_ref, loc_sem, xl_sem, k_ss, k_rs, v_ss, v_rs, vr_ss, x_ss, x_rs,
    dv_ss, dv_rs, dk_ss, dk_rs, vg_ss, vg_rs, p_ss, p_rs,
    r_ss, r_rs, l_ss, l_rs, f_ss, f_rs, held,
):
    s = lax.axis_index("seq")
    f = lax.axis_index("fsdp")
    rows = q.shape[0]
    width = wfin.shape[0]
    cut = width // cuts
    kvw = groups * HEAD_SIZE
    keys = (BACK + 1) * rows
    couples = groups // 2
    units = cuts * couples
    chunks = units * SUBS
    sub_rows = cut // SUBS
    core = s % 2
    z = s // 2
    depth = n_s // 2
    sibling = s + 1 - 2 * core
    even = core == 0
    last = z == depth - 1
    scale = 1.0 / math.sqrt(HEAD_SIZE)

    def remote(src, dst, ss, rs, to_s, to_f):
        return pltpu.make_async_remote_copy(
            src_ref=src, dst_ref=dst, send_sem=ss, recv_sem=rs,
            device_id={"seq": to_s, "fsdp": to_f}, device_id_type=MESH,
        )

    def x_cols(to, r):
        return pl.ds(pl.multiple_of(to * width + r * cut, 128), cut)

    local = [
        pltpu.make_async_copy(q_hbm.at[0], q, loc_sem.at[0]),
        pltpu.make_async_copy(k_hbm.at[0], kwin.at[BACK], loc_sem.at[1]),
        pltpu.make_async_copy(g_hbm.at[0], g, loc_sem.at[2]),
        pltpu.make_async_copy(v_hbm.at[0], vwin.at[BACK], loc_sem.at[3]),
    ]

    def own_x(r):
        return pltpu.make_async_copy(x_hbm.at[0, :, x_cols(f, r)], xg.at[r, f], xl_sem.at[r])

    doc_copy = pltpu.make_async_copy(doc_hbm, doc_ref, loc_sem.at[4])
    doc_copy.start()
    for copy in local + [own_x(r) for r in range(cuts)]:
        copy.start()

    barrier = pltpu.get_barrier_semaphore()
    for d in range(1, BACK + 1):
        @pl.when(s >= d)
        def _():
            pl.semaphore_signal(
                barrier, inc=1, device_id={"seq": s - d, "fsdp": f}, device_id_type=MESH
            )

        @pl.when(s + d < n_s)
        def _():
            pl.semaphore_signal(
                barrier, inc=1, device_id={"seq": s + d, "fsdp": f}, device_id_type=MESH
            )
    for j in range(1, n_f):
        pl.semaphore_signal(
            barrier, inc=1, device_id={"seq": s, "fsdp": (f + j) % n_f}, device_id_type=MESH
        )

    doc_copy.wait()

    def doc_of(block):
        end = jnp.int32(0)
        doc = jnp.int32(0)
        for i in range(doc_ref.shape[1]):
            end = end + doc_ref[0, i]
            doc = doc + jnp.where(block >= end, 1, 0)
        return doc

    mine = doc_of(s)
    for d in range(1, BACK + 1):
        seen = jnp.logical_and(doc_of(s - d) == mine, s >= d)
        level = jnp.where(seen, 0.0, -jnp.inf).astype(F32)
        bias[(BACK - d) * rows : (BACK - d + 1) * rows, :] = jnp.full(
            (rows, PAIR * rows), level, F32
        )
    key_at = lax.broadcasted_iota(jnp.int32, (rows, PAIR * rows), 0)
    query_at = lax.broadcasted_iota(jnp.int32, (rows, PAIR * rows), 1) % rows
    bias[BACK * rows :, :] = jnp.where(key_at <= query_at, 0.0, -jnp.inf).astype(F32)

    for d in range(1, BACK + 1):
        @pl.when(s < d)
        def _():
            kwin[BACK - d] = jnp.zeros((rows, kvw), BF16)
            vwin[BACK - d] = jnp.zeros((rows, kvw), BF16)

        @pl.when(s + d >= n_s)
        def _():
            dv_recv[d - 1] = jnp.zeros((rows, kvw), BF16)
            dk_recv[d - 1] = jnp.zeros((rows, kvw), BF16)

    @pl.when(z == 0)
    def _():
        left_recv[...] = jnp.zeros_like(left_recv)

    @pl.when(z == depth - 1)
    def _():
        right_recv[...] = jnp.zeros_like(right_recv)

    one = lambda c: jnp.where(c, 1, 0)
    pl.semaphore_wait(
        barrier, n_f - 1 + one(s >= 1) + one(s >= 2) + one(s + 1 < n_s) + one(s + 2 < n_s)
    )

    def group_cols(i):
        return pl.ds(pl.multiple_of(i * HEAD_SIZE, HEAD_SIZE), HEAD_SIZE)

    has_next = s + 1 < n_s
    even_two = jnp.logical_and(even, s + 2 < n_s)
    relays = jnp.logical_and(even, s >= 1)

    def k_copy(d, i):
        return remote(
            k_hbm.at[0, :, group_cols(i)], kwin.at[BACK - d, :, group_cols(i)],
            k_ss.at[d - 1, i], k_rs.at[d - 1, i], s + d, f,
        )

    def v_copy(d):
        return remote(
            v_hbm.at[0], vwin.at[BACK - d], v_ss.at[d - 1], v_rs.at[d - 1], s + d, f
        )

    def v_relay():
        return remote(vwin.at[BACK - 1], vwin.at[BACK - 2], vr_ss.at[0], v_rs.at[1], s + 1, f)

    def x_copy(r, j):
        to = (f + j) % n_f
        return remote(
            x_hbm.at[0, :, x_cols(to, r)], xg.at[r, f], x_ss.at[r, j], x_rs.at[r, j], s, to
        )

    def x_start(r):
        for j in range(1, n_f):
            x_copy(r, j).start()

    for i in range(groups):
        @pl.when(has_next)
        def _():
            k_copy(1, i).start()

        @pl.when(s + 2 < n_s)
        def _():
            k_copy(2, i).start()

    @pl.when(has_next)
    def _():
        v_copy(1).start()

    @pl.when(even_two)
    def _():
        v_copy(2).start()

    for r in range(EARLY):
        x_start(r)

    for copy in local[:3]:
        copy.wait()

    def back_copy(send, recv, ss, rs, d, i):
        return remote(
            send.at[d - 1, :, group_cols(i)], recv.at[d - 1, :, group_cols(i)],
            ss.at[d - 1, i], rs.at[d - 1, i], s - d, f,
        )

    def pair_of(ref, i, j):
        first = (i * heads + j * PAIR) * HEAD_SIZE
        return jnp.concatenate(
            [
                ref[:, pl.ds(pl.multiple_of(first + n * HEAD_SIZE, HEAD_SIZE), HEAD_SIZE)]
                for n in range(PAIR)
            ],
            axis=0,
        )

    def give_back(total, own, send, recv, ss, rs, i):
        own[:, group_cols(i)] = total[BACK * rows :]
        for d in range(1, BACK + 1):
            send[d - 1, :, group_cols(i)] = total[(BACK - d) * rows : (BACK - d + 1) * rows].astype(
                BF16
            )

            @pl.when(s >= d)
            def _():
                back_copy(send, recv, ss, rs, d, i).start()

    def first_pass(i):
        @pl.when(s >= 1)
        def _():
            k_copy(1, i).wait_recv()

        @pl.when(s >= 2)
        def _():
            k_copy(2, i).wait_recv()

        k_group = kwin[:, :, group_cols(i)].reshape(keys, HEAD_SIZE)
        total = jnp.zeros((keys, HEAD_SIZE), F32)
        for j in range(heads // PAIR):
            scores = matmul(k_group, pair_of(q, i, j), 1, 1)
            scores = scores * (scale * math.log2(math.e)) + bias[...]
            exps = jnp.exp2(scores - jnp.max(scores, axis=0, keepdims=True))
            p = exps * (1.0 / jnp.sum(exps, axis=0, keepdims=True))
            probs[i, j] = p
            total = total + matmul(p.astype(BF16), pair_of(g, i, j), 1, 0)
        give_back(total, dv_own, dv_send, dv_recv, dv_ss, dv_rs, i)

    def second_part(i, j, k_group, v_group, k_turned):
        p = probs[i, j]
        d_probs = matmul(v_group, pair_of(g, i, j), 1, 1)
        deltas = jnp.sum(p * d_probs, axis=0, keepdims=True)
        d_scores = (p * (d_probs - deltas)).astype(BF16)
        turned = (matmul(k_turned, d_scores, 1, 0) * scale).T.astype(BF16)
        first = (i * heads + j * PAIR) * HEAD_SIZE
        for n in range(PAIR):
            cols = pl.ds(pl.multiple_of(first + n * HEAD_SIZE, HEAD_SIZE), HEAD_SIZE)
            dq_out[0, :, cols] = turned[n * rows : (n + 1) * rows]
        return matmul(d_scores, pair_of(q, i, j), 1, 0)

    def second_pass(i):
        k_group = kwin[:, :, group_cols(i)].reshape(keys, HEAD_SIZE)
        v_group = vwin[:, :, group_cols(i)].reshape(keys, HEAD_SIZE)
        k_turned = k_group.T
        total = jnp.zeros((keys, HEAD_SIZE), F32)
        for j in range(heads // PAIR):
            total = total + second_part(i, j, k_group, v_group, k_turned)
        give_back(total * scale, dk_own, dk_send, dk_recv, dk_ss, dk_rs, i)

    def second_piece(i, j):
        @pl.when(j == 0)
        def _():
            held[...] = jnp.zeros_like(held)

        k_group = kwin[:, :, group_cols(i)].reshape(keys, HEAD_SIZE)
        v_group = vwin[:, :, group_cols(i)].reshape(keys, HEAD_SIZE)
        held[...] = held[...] + second_part(i, j, k_group, v_group, k_group.T)

        @pl.when(j == heads // PAIR - 1)
        def _():
            give_back(held[...] * scale, dk_own, dk_send, dk_recv, dk_ss, dk_rs, i)

    def vg_copy(i, j):
        return remote(
            vgb.at[f, :, group_cols(i)], vgb.at[f, :, group_cols(i)], vg_ss.at[i, j], vg_rs.at[i, j],
            s, (f + j) % n_f,
        )

    def collect(own, recv, send, ss, rs, i):
        for d in range(1, BACK + 1):
            @pl.when(s + d < n_s)
            def _():
                back_copy(send, recv, ss, rs, d, i).wait_recv()
        cols = group_cols(i)
        total = own[:, cols]
        for d in range(1, BACK + 1):
            total = total + recv[d - 1, :, cols].astype(F32)
        return total.astype(BF16)

    def value(i):
        done = collect(dv_own, dv_recv, dv_send, dv_ss, dv_rs, i)
        vgb[f, :, group_cols(i)] = done
        vg_out[0, :, group_cols(i)] = done
        for j in range(1, n_f):
            vg_copy(i, j).start()

    def place_of(u):
        early = u < 2 * couples
        return jnp.where(early, u % 2, u // couples), jnp.where(early, u // 2, u % couples)

    def pair_copy(u):
        return remote(pair_send.at[u], pair_recv.at[u], p_ss.at[u], p_rs.at[u], sibling, f)

    def weight_unit(u):
        r, p = place_of(jnp.int32(u))

        @pl.when(r == 0)
        def _():
            for n in range(2):
                for j in range(1, n_f):
                    vg_copy(2 * p + n, j).wait_recv()

        @pl.when(p == 0)
        def _():
            own_x(r).wait()
            for j in range(1, n_f):
                x_copy(r, j).wait_recv()

        cols = pl.ds(pl.multiple_of(2 * p * HEAD_SIZE, 2 * HEAD_SIZE), 2 * HEAD_SIZE)
        values = vgb[:, :, cols].reshape(n_f * rows, 2 * HEAD_SIZE)
        part = matmul(xg[r].reshape(n_f * rows, cut), values, 0, 0)
        first, second = part[:, :HEAD_SIZE], part[:, HEAD_SIZE:]
        w_own[u] = jnp.where(even, first, second)
        pair_send[u] = jnp.where(even, second, first).astype(BF16)
        pair_copy(u).start()

    def right_copy(c):
        return remote(right_send.at[c], left_recv.at[c], r_ss.at[c], r_rs.at[c], s + 2, f)

    def left_copy(c):
        return remote(left_send.at[c], right_recv.at[c], l_ss.at[c], l_rs.at[c], s - 2, f)

    def place(c, side):
        r, p = place_of(c // SUBS)
        at = r * cut + (c % SUBS) * sub_rows
        return wfin.at[
            pl.ds(pl.multiple_of(at, sub_rows), sub_rows), group_cols(2 * p + side)
        ]

    def final_copy(c):
        return remote(place(c, core), place(c, core), f_ss.at[c], f_rs.at[c], sibling, f)

    def own_chunk(c):
        return w_own[c // SUBS, pl.ds(pl.multiple_of((c % SUBS) * sub_rows, sub_rows), sub_rows), :]

    token_count = n_f * n_s * rows

    def step(t, carry):
        to_right = t - SLACK * z - LATER
        to_left = t - SLACK * (depth - 1 - z)
        done = jnp.minimum(to_right, to_left)

        def inside(c):
            return jnp.logical_and(c >= 0, c < chunks)

        @pl.when(jnp.logical_and(inside(to_left), z < depth - 1))
        def _():
            left_copy(to_left).wait_recv()

        @pl.when(jnp.logical_and(inside(to_left), z > 0))
        def _():
            left_send[to_left] = (own_chunk(to_left) + right_recv[to_left].astype(F32)).astype(BF16)
            left_copy(to_left).start()

        @pl.when(jnp.logical_and(inside(to_right), z > 0))
        def _():
            right_copy(to_right).wait_recv()

        @pl.when(jnp.logical_and(inside(to_right), z < depth - 1))
        def _():
            right_send[to_right] = (own_chunk(to_right) + left_recv[to_right].astype(F32)).astype(
                BF16
            )
            right_copy(to_right).start()

        @pl.when(inside(done))
        def _():
            total = own_chunk(done) + left_recv[done].astype(F32) + right_recv[done].astype(F32)
            place(done, core)[...] = (total * (1.0 / math.sqrt(token_count))).astype(BF16)
            final_copy(done).start()

        return carry

    lag = jnp.where(last, 1, 3)
    ready = groups - lag

    def first_loop(i, carry):
        @pl.when(jnp.logical_and(i >= lag, jnp.logical_not(last)))
        def _():
            value(i - lag)

        first_pass(i)

        @pl.when(jnp.logical_and(i >= lag, last))
        def _():
            value(i - lag)

        return carry

    lax.fori_loop(0, groups, first_loop, 0)

    local[3].wait()
    @pl.when(s >= 1)
    def _():
        v_copy(1).wait_recv()

    @pl.when(relays)
    def _():
        v_relay().start()

    @pl.when(s >= 2)
    def _():
        v_copy(2).wait_recv()

    early = jnp.where(last, 0, jnp.where(z == depth - 2, groups - HELD, groups))

    def value_loop(k, carry):
        @pl.when(k < groups - 1)
        def _():
            value(k)

        @pl.when(jnp.logical_and(k >= 1, k <= early))
        def _():
            second_pass(k - 1)

        @pl.when(k == groups - 1)
        def _():
            value(k)
            for r in range(EARLY, cuts):
                x_start(r)

        return carry

    lax.fori_loop(ready, groups, value_loop, 0)

    def settle(c, carry):
        other = remote(place(c, 1 - core), place(c, 1 - core), f_ss.at[c], f_rs.at[c], sibling, f)
        other.wait_recv()
        final_copy(c).wait_send()

        @pl.when(z < depth - 1)
        def _():
            right_copy(c).wait_send()

        @pl.when(z > 0)
        def _():
            left_copy(c).wait_send()

        return carry

    def tidy():
        for i in range(groups):
            dk_out[0, :, i * HEAD_SIZE : (i + 1) * HEAD_SIZE] = collect(
                dk_own, dk_recv, dk_send, dk_ss, dk_rs, i
            )

        @pl.when(has_next)
        def _():
            v_copy(1).wait_send()
            for i in range(groups):
                k_copy(1, i).wait_send()

        @pl.when(s + 2 < n_s)
        def _():
            for i in range(groups):
                k_copy(2, i).wait_send()

        @pl.when(even_two)
        def _():
            v_copy(2).wait_send()

        @pl.when(relays)
        def _():
            v_relay().wait_send()

        for d in range(1, BACK + 1):
            @pl.when(s >= d)
            def _():
                for i in range(groups):
                    back_copy(dv_send, dv_recv, dv_ss, dv_rs, d, i).wait_send()
                    back_copy(dk_send, dk_recv, dk_ss, dk_rs, d, i).wait_send()
        for j in range(1, n_f):
            for r in range(cuts):
                x_copy(r, j).wait_send()
            for i in range(groups):
                vg_copy(i, j).wait_send()
        for u in range(units):
            pair_copy(u).wait_send()

    shift = jnp.minimum(SLACK * (depth - 1 - z), SLACK * z + LATER)

    def second_loop(i, carry):
        second_pass(i)
        return carry

    total = chunks + SLACK * (depth - 1) + LATER
    parts = heads // PAIR

    def line(t, carry):
        own = t - shift
        u = own // SUBS

        @pl.when(jnp.logical_and(own % SUBS == 0, jnp.logical_and(own >= 0, u < units)))
        def _():
            pair_copy(u).wait_recv()
            w_own[u] = w_own[u] + pair_recv[u].astype(F32)

        step(t, carry)

        @pl.when(jnp.logical_and(own % SUBS == 0, jnp.logical_and(own >= 0, u + AHEAD < units)))
        def _():
            weight_unit(u + AHEAD)

        behind = jnp.minimum(t - SLACK * z - LATER, t - SLACK * (depth - 1 - z)) - BEHIND

        @pl.when(jnp.logical_and(behind >= 0, behind < chunks - BEHIND))
        def _():
            settle(behind, 0)

        @pl.when(t == total - BEHIND)
        def _():
            tidy()

        @pl.when(jnp.logical_and(own == chunks - 1, last))
        def _():
            lax.fori_loop(early, groups, second_loop, 0)

        piece = (own - FROM) // EVERY
        turn = jnp.logical_and(own >= FROM, (own - FROM) % EVERY == 0)

        @pl.when(jnp.logical_and(jnp.logical_and(turn, z == depth - 2), piece < HELD * parts))
        def _():
            second_piece(groups - HELD + piece // parts, piece % parts)

        return carry

    for u in range(AHEAD):
        weight_unit(u)
    lax.fori_loop(jnp.where(z < depth - 2, groups - 1, groups), groups, second_loop, 0)
    lax.fori_loop(0, total, line, 0)

    lax.fori_loop(chunks - BEHIND, chunks, settle, 0)


def settle_outputs(*refs):
    sources, outs, sems = refs[:4], refs[4:8], refs[8]
    saves = [pltpu.make_async_copy(sources[i], outs[i], sems.at[i]) for i in range(4)]
    for save in saves:
        save.start()
    for save in saves:
        save.wait()


def shards(n_s, n_f, layer_inputs, queries, key_states, value_states, output_gradient, doc_blocks):
    rows = queries.shape[1]
    kvw = key_states.shape[2]
    groups = kvw // HEAD_SIZE
    heads = queries.shape[2] // kvw
    width = layer_inputs.shape[2] // n_f
    cuts = 4 if width % (4 * 128) == 0 else 2
    cut = width // cuts
    units = cuts * (groups // 2)
    chunks = units * SUBS
    keys = (BACK + 1) * rows
    V = pltpu.VMEM
    D = pltpu.SemaphoreType.DMA
    strip = V((chunks, cut // SUBS, HEAD_SIZE), BF16)
    scratch = [
        V((rows, queries.shape[2]), BF16),
        V((rows, queries.shape[2]), BF16),
        V((BACK + 1, rows, kvw), BF16),
        V((BACK + 1, rows, kvw), BF16),
        V((cuts, n_f, rows, cut), BF16),
        V((groups, heads // PAIR, keys, PAIR * rows), F32),
        V((keys, PAIR * rows), F32),
        V((rows, kvw), F32),
        V((BACK, rows, kvw), BF16),
        V((BACK, rows, kvw), BF16),
        V((rows, kvw), F32),
        V((BACK, rows, kvw), BF16),
        V((BACK, rows, kvw), BF16),
        V((n_f, rows, kvw), BF16),
        V((units, cut, HEAD_SIZE), F32),
        V((units, cut, HEAD_SIZE), BF16),
        V((units, cut, HEAD_SIZE), BF16),
        strip, strip, strip, strip,
        pltpu.SMEM(doc_blocks.shape, jnp.int32),
        D((5,)), D((cuts,)),
        D((BACK, groups)), D((BACK, groups)),
        D((BACK,)), D((BACK,)), D((1,)), D((cuts, n_f)), D((cuts, n_f)),
        D((BACK, groups)), D((BACK, groups)), D((BACK, groups)), D((BACK, groups)),
        D((groups, n_f)), D((groups, n_f)), D((units,)), D((units,)),
        D((chunks,)), D((chunks,)), D((chunks,)), D((chunks,)), D((chunks,)), D((chunks,)),
        V((keys, HEAD_SIZE), F32),
    ]
    far = pl.BlockSpec(memory_space=pltpu.HBM)
    near = pl.BlockSpec(memory_space=pltpu.VMEM)
    out_shape = [
        jax.ShapeDtypeStruct(queries.shape, BF16),
        jax.ShapeDtypeStruct(key_states.shape, BF16),
        jax.ShapeDtypeStruct(key_states.shape, BF16),
        jax.ShapeDtypeStruct((width, kvw), BF16),
    ]
    held = [
        pltpu.with_memory_space_constraint(a, pltpu.HBM)
        for a in (doc_blocks, layer_inputs, queries, key_states, value_states, output_gradient)
    ]
    made = pl.pallas_call(
        functools.partial(kernel, n_s, n_f, groups, heads, cuts),
        out_shape=[pltpu.VMEM(o.shape, o.dtype) for o in out_shape],
        in_specs=[far] * 6,
        out_specs=[near] * 4,
        scratch_shapes=scratch,
        compiler_params=pltpu.CompilerParams(
            collective_id=0, has_side_effects=True, vmem_limit_bytes=VMEM_LIMIT
        ),
    )(*held)
    return tuple(
        pl.pallas_call(
            settle_outputs,
            out_shape=out_shape,
            in_specs=[near] * 4,
            out_specs=[far] * 4,
            scratch_shapes=[D((4,))],
            compiler_params=pltpu.CompilerParams(vmem_limit_bytes=SMALL_LIMIT),
        )(*made)
    )


def solution(mesh):
    sizes = dict(mesh.shape)
    return jax.shard_map(
        functools.partial(shards, sizes["seq"], sizes["fsdp"]),
        mesh=mesh,
        in_specs=(P("fsdp", "seq", None),) * 5 + (P("fsdp", None),),
        out_specs=(P("fsdp", "seq", None),) * 3 + (P("fsdp", None),),
        check_vma=False,
    )
```

```python
import functools
import math

import jax
import jax.numpy as jnp
from jax import lax
from jax.experimental import pallas as pl
from jax.experimental.pallas import tpu as pltpu
from jax.sharding import PartitionSpec as P

HEAD_SIZE = 128
BLOCK = 128
BACK = 2
PAIR = 2
SUBS = 2
EARLY = 2
SLACK = 5
LATER = 4
AHEAD = 1
HELD = 2
FROM = 5
EVERY = 2
BEHIND = 6
VMEM_LIMIT = 40 * 1024 * 1024
SMALL_LIMIT = 8 * 1024 * 1024
MESH = pl.DeviceIdType.MESH
F32 = jnp.float32
BF16 = jnp.bfloat16


def matmul(a, b, ca, cb):
    return lax.dot_general(a, b, (((ca,), (cb,)), ((), ())), preferred_element_type=F32)


def kernel(
    n_s, n_f, groups, heads, cuts,
    doc_hbm, x_hbm, q_hbm, k_hbm, v_hbm, g_hbm,
    dq_out, dk_out, vg_out, wfin,
    q, g, kwin, vwin, xg, probs, bias,
    dv_own, dv_send, dv_recv, dk_own, dk_send, dk_recv, vgb,
    w_own, pair_send, pair_recv, right_send, left_recv, left_send, right_recv,
    doc_ref, loc_sem, xl_sem, k_ss, k_rs, v_ss, v_rs, vr_ss, x_ss, x_rs,
    dv_ss, dv_rs, dk_ss, dk_rs, vg_ss, vg_rs, p_ss, p_rs,
    r_ss, r_rs, l_ss, l_rs, f_ss, f_rs, held,
):
    s = lax.axis_index("seq")
    f = lax.axis_index("fsdp")
    rows = q.shape[0]
    width = wfin.shape[0]
    cut = width // cuts
    kvw = groups * HEAD_SIZE
    keys = (BACK + 1) * rows
    couples = groups // 2
    units = cuts * couples
    chunks = units * SUBS
    sub_rows = cut // SUBS
    core = s % 2
    z = s // 2
    depth = n_s // 2
    sibling = s + 1 - 2 * core
    even = core == 0
    last = z == depth - 1
    scale = 1.0 / math.sqrt(HEAD_SIZE)

    side = math.isqrt(n_f) if math.isqrt(n_f) ** 2 == n_f else n_f
    peers = sorted(range(1, n_f), key=lambda j: -(j // side > 0) - (j % side > 0))

    def peer(j):
        return (f // side + j // side) % (n_f // side) * side + (f % side + j % side) % side

    def remote(src, dst, ss, rs, to_s, to_f):
        return pltpu.make_async_remote_copy(
            src_ref=src, dst_ref=dst, send_sem=ss, recv_sem=rs,
            device_id={"seq": to_s, "fsdp": to_f}, device_id_type=MESH,
        )

    def x_cols(to, r):
        return pl.ds(pl.multiple_of(to * width + r * cut, 128), cut)

    local = [
        pltpu.make_async_copy(q_hbm.at[0], q, loc_sem.at[0]),
        pltpu.make_async_copy(k_hbm.at[0], kwin.at[BACK], loc_sem.at[1]),
        pltpu.make_async_copy(g_hbm.at[0], g, loc_sem.at[2]),
        pltpu.make_async_copy(v_hbm.at[0], vwin.at[BACK], loc_sem.at[3]),
    ]

    def own_x(r):
        return pltpu.make_async_copy(x_hbm.at[0, :, x_cols(f, r)], xg.at[r, f], xl_sem.at[r])

    doc_copy = pltpu.make_async_copy(doc_hbm, doc_ref, loc_sem.at[4])
    doc_copy.start()
    for copy in local + [own_x(r) for r in range(cuts)]:
        copy.start()

    barrier = pltpu.get_barrier_semaphore()
    for d in range(1, BACK + 1):
        @pl.when(s >= d)
        def _():
            pl.semaphore_signal(
                barrier, inc=1, device_id={"seq": s - d, "fsdp": f}, device_id_type=MESH
            )

        @pl.when(s + d < n_s)
        def _():
            pl.semaphore_signal(
                barrier, inc=1, device_id={"seq": s + d, "fsdp": f}, device_id_type=MESH
            )
    for j in peers:
        pl.semaphore_signal(
            barrier, inc=1, device_id={"seq": s, "fsdp": peer(j)}, device_id_type=MESH
        )

    doc_copy.wait()

    def doc_of(block):
        end = jnp.int32(0)
        doc = jnp.int32(0)
        for i in range(doc_ref.shape[1]):
            end = end + doc_ref[0, i]
            doc = doc + jnp.where(block >= end, 1, 0)
        return doc

    mine = doc_of(s)
    for d in range(1, BACK + 1):
        seen = jnp.logical_and(doc_of(s - d) == mine, s >= d)
        level = jnp.where(seen, 0.0, -jnp.inf).astype(F32)
        bias[(BACK - d) * rows : (BACK - d + 1) * rows, :] = jnp.full(
            (rows, PAIR * rows), level, F32
        )
    key_at = lax.broadcasted_iota(jnp.int32, (rows, PAIR * rows), 0)
    query_at = lax.broadcasted_iota(jnp.int32, (rows, PAIR * rows), 1) % rows
    bias[BACK * rows :, :] = jnp.where(key_at <= query_at, 0.0, -jnp.inf).astype(F32)

    for d in range(1, BACK + 1):
        @pl.when(s < d)
        def _():
            kwin[BACK - d] = jnp.zeros((rows, kvw), BF16)
            vwin[BACK - d] = jnp.zeros((rows, kvw), BF16)

        @pl.when(s + d >= n_s)
        def _():
            dv_recv[d - 1] = jnp.zeros((rows, kvw), BF16)
            dk_recv[d - 1] = jnp.zeros((rows, kvw), BF16)

    @pl.when(z == 0)
    def _():
        left_recv[...] = jnp.zeros_like(left_recv)

    @pl.when(z == depth - 1)
    def _():
        right_recv[...] = jnp.zeros_like(right_recv)

    one = lambda c: jnp.where(c, 1, 0)
    pl.semaphore_wait(
        barrier, n_f - 1 + one(s >= 1) + one(s >= 2) + one(s + 1 < n_s) + one(s + 2 < n_s)
    )

    def group_cols(i):
        return pl.ds(pl.multiple_of(i * HEAD_SIZE, HEAD_SIZE), HEAD_SIZE)

    has_next = s + 1 < n_s
    even_two = jnp.logical_and(even, s + 2 < n_s)
    relays = jnp.logical_and(even, s >= 1)

    def k_copy(d, i):
        return remote(
            k_hbm.at[0, :, group_cols(i)], kwin.at[BACK - d, :, group_cols(i)],
            k_ss.at[d - 1, i], k_rs.at[d - 1, i], s + d, f,
        )

    def v_copy(d):
        return remote(
            v_hbm.at[0], vwin.at[BACK - d], v_ss.at[d - 1], v_rs.at[d - 1], s + d, f
        )

    def v_relay():
        return remote(vwin.at[BACK - 1], vwin.at[BACK - 2], vr_ss.at[0], v_rs.at[1], s + 1, f)

    def x_copy(r, j):
        to = peer(j)
        return remote(
            x_hbm.at[0, :, x_cols(to, r)], xg.at[r, f], x_ss.at[r, j], x_rs.at[r, j], s, to
        )

    def x_start(r):
        for j in peers:
            x_copy(r, j).start()

    for i in range(groups):
        @pl.when(has_next)
        def _():
            k_copy(1, i).start()

        @pl.when(s + 2 < n_s)
        def _():
            k_copy(2, i).start()

    @pl.when(has_next)
    def _():
        v_copy(1).start()

    @pl.when(even_two)
    def _():
        v_copy(2).start()

    for r in range(EARLY):
        x_start(r)

    for copy in local[:3]:
        copy.wait()

    def back_copy(send, recv, ss, rs, d, i):
        return remote(
            send.at[d - 1, :, group_cols(i)], recv.at[d - 1, :, group_cols(i)],
            ss.at[d - 1, i], rs.at[d - 1, i], s - d, f,
        )

    def pair_of(ref, i, j):
        first = (i * heads + j * PAIR) * HEAD_SIZE
        return jnp.concatenate(
            [
                ref[:, pl.ds(pl.multiple_of(first + n * HEAD_SIZE, HEAD_SIZE), HEAD_SIZE)]
                for n in range(PAIR)
            ],
            axis=0,
        )

    def give_back(total, own, send, recv, ss, rs, i):
        own[:, group_cols(i)] = total[BACK * rows :]
        for d in range(1, BACK + 1):
            send[d - 1, :, group_cols(i)] = total[(BACK - d) * rows : (BACK - d + 1) * rows].astype(
                BF16
            )

            @pl.when(s >= d)
            def _():
                back_copy(send, recv, ss, rs, d, i).start()

    def first_pass(i):
        @pl.when(s >= 1)
        def _():
            k_copy(1, i).wait_recv()

        @pl.when(s >= 2)
        def _():
            k_copy(2, i).wait_recv()

        k_group = kwin[:, :, group_cols(i)].reshape(keys, HEAD_SIZE)
        total = jnp.zeros((keys, HEAD_SIZE), F32)
        for j in range(heads // PAIR):
            scores = matmul(k_group, pair_of(q, i, j), 1, 1)
            scores = scores * (scale * math.log2(math.e)) + bias[...]
            exps = jnp.exp2(scores - jnp.max(scores, axis=0, keepdims=True))
            p = exps * (1.0 / jnp.sum(exps, axis=0, keepdims=True))
            probs[i, j] = p
            total = total + matmul(p.astype(BF16), pair_of(g, i, j), 1, 0)
        give_back(total, dv_own, dv_send, dv_recv, dv_ss, dv_rs, i)

    def second_part(i, j, k_group, v_group, k_turned):
        p = probs[i, j]
        d_probs = matmul(v_group, pair_of(g, i, j), 1, 1)
        deltas = jnp.sum(p * d_probs, axis=0, keepdims=True)
        d_scores = (p * (d_probs - deltas)).astype(BF16)
        turned = (matmul(k_turned, d_scores, 1, 0) * scale).T.astype(BF16)
        first = (i * heads + j * PAIR) * HEAD_SIZE
        for n in range(PAIR):
            cols = pl.ds(pl.multiple_of(first + n * HEAD_SIZE, HEAD_SIZE), HEAD_SIZE)
            dq_out[0, :, cols] = turned[n * rows : (n + 1) * rows]
        return matmul(d_scores, pair_of(q, i, j), 1, 0)

    def second_pass(i):
        k_group = kwin[:, :, group_cols(i)].reshape(keys, HEAD_SIZE)
        v_group = vwin[:, :, group_cols(i)].reshape(keys, HEAD_SIZE)
        k_turned = k_group.T
        total = jnp.zeros((keys, HEAD_SIZE), F32)
        for j in range(heads // PAIR):
            total = total + second_part(i, j, k_group, v_group, k_turned)
        give_back(total * scale, dk_own, dk_send, dk_recv, dk_ss, dk_rs, i)

    def second_piece(i, j):
        @pl.when(j == 0)
        def _():
            held[...] = jnp.zeros_like(held)

        k_group = kwin[:, :, group_cols(i)].reshape(keys, HEAD_SIZE)
        v_group = vwin[:, :, group_cols(i)].reshape(keys, HEAD_SIZE)
        held[...] = held[...] + second_part(i, j, k_group, v_group, k_group.T)

        @pl.when(j == heads // PAIR - 1)
        def _():
            give_back(held[...] * scale, dk_own, dk_send, dk_recv, dk_ss, dk_rs, i)

    def vg_copy(i, j):
        return remote(
            vgb.at[f, :, group_cols(i)], vgb.at[f, :, group_cols(i)], vg_ss.at[i, j], vg_rs.at[i, j],
            s, peer(j),
        )

    def collect(own, recv, send, ss, rs, i):
        for d in range(1, BACK + 1):
            @pl.when(s + d < n_s)
            def _():
                back_copy(send, recv, ss, rs, d, i).wait_recv()
        cols = group_cols(i)
        total = own[:, cols]
        for d in range(1, BACK + 1):
            total = total + recv[d - 1, :, cols].astype(F32)
        return total.astype(BF16)

    def value(i):
        done = collect(dv_own, dv_recv, dv_send, dv_ss, dv_rs, i)
        vgb[f, :, group_cols(i)] = done
        vg_out[0, :, group_cols(i)] = done
        for j in peers:
            vg_copy(i, j).start()

    def place_of(u):
        early = u < 2 * couples
        return jnp.where(early, u % 2, u // couples), jnp.where(early, u // 2, u % couples)

    def pair_copy(u):
        return remote(pair_send.at[u], pair_recv.at[u], p_ss.at[u], p_rs.at[u], sibling, f)

    def weight_unit(u):
        r, p = place_of(jnp.int32(u))

        @pl.when(r == 0)
        def _():
            for n in range(2):
                for j in peers:
                    vg_copy(2 * p + n, j).wait_recv()

        @pl.when(p == 0)
        def _():
            own_x(r).wait()
            for j in peers:
                x_copy(r, j).wait_recv()

        cols = pl.ds(pl.multiple_of(2 * p * HEAD_SIZE, 2 * HEAD_SIZE), 2 * HEAD_SIZE)
        values = vgb[:, :, cols].reshape(n_f * rows, 2 * HEAD_SIZE)
        part = matmul(xg[r].reshape(n_f * rows, cut), values, 0, 0)
        first, second = part[:, :HEAD_SIZE], part[:, HEAD_SIZE:]
        w_own[u] = jnp.where(even, first, second)
        pair_send[u] = jnp.where(even, second, first).astype(BF16)
        pair_copy(u).start()

    def right_copy(c):
        return remote(right_send.at[c], left_recv.at[c], r_ss.at[c], r_rs.at[c], s + 2, f)

    def left_copy(c):
        return remote(left_send.at[c], right_recv.at[c], l_ss.at[c], l_rs.at[c], s - 2, f)

    def place(c, side):
        r, p = place_of(c // SUBS)
        at = r * cut + (c % SUBS) * sub_rows
        return wfin.at[
            pl.ds(pl.multiple_of(at, sub_rows), sub_rows), group_cols(2 * p + side)
        ]

    def final_copy(c):
        return remote(place(c, core), place(c, core), f_ss.at[c], f_rs.at[c], sibling, f)

    def own_chunk(c):
        return w_own[c // SUBS, pl.ds(pl.multiple_of((c % SUBS) * sub_rows, sub_rows), sub_rows), :]

    token_count = n_f * n_s * rows

    def step(t, carry):
        to_right = t - SLACK * z - LATER
        to_left = t - SLACK * (depth - 1 - z)
        done = jnp.minimum(to_right, to_left)

        def inside(c):
            return jnp.logical_and(c >= 0, c < chunks)

        @pl.when(jnp.logical_and(inside(to_left), z < depth - 1))
        def _():
            left_copy(to_left).wait_recv()

        @pl.when(jnp.logical_and(inside(to_left), z > 0))
        def _():
            left_send[to_left] = (own_chunk(to_left) + right_recv[to_left].astype(F32)).astype(BF16)
            left_copy(to_left).start()

        @pl.when(jnp.logical_and(inside(to_right), z > 0))
        def _():
            right_copy(to_right).wait_recv()

        @pl.when(jnp.logical_and(inside(to_right), z < depth - 1))
        def _():
            right_send[to_right] = (own_chunk(to_right) + left_recv[to_right].astype(F32)).astype(
                BF16
            )
            right_copy(to_right).start()

        @pl.when(inside(done))
        def _():
            total = own_chunk(done) + left_recv[done].astype(F32) + right_recv[done].astype(F32)
            place(done, core)[...] = (total * (1.0 / math.sqrt(token_count))).astype(BF16)
            final_copy(done).start()

        return carry

    lag = jnp.where(last, 1, 3)
    ready = groups - lag

    def first_loop(i, carry):
        @pl.when(jnp.logical_and(i >= lag, jnp.logical_not(last)))
        def _():
            value(i - lag)

        first_pass(i)

        @pl.when(jnp.logical_and(i >= lag, last))
        def _():
            value(i - lag)

        return carry

    lax.fori_loop(0, groups, first_loop, 0)

    local[3].wait()
    @pl.when(s >= 1)
    def _():
        v_copy(1).wait_recv()

    @pl.when(relays)
    def _():
        v_relay().start()

    @pl.when(s >= 2)
    def _():
        v_copy(2).wait_recv()

    early = jnp.where(last, 0, jnp.where(z == depth - 2, groups - HELD, groups))

    def value_loop(k, carry):
        @pl.when(k < groups - 1)
        def _():
            value(k)

        @pl.when(jnp.logical_and(k >= 1, k <= early))
        def _():
            second_pass(k - 1)

        @pl.when(k == groups - 1)
        def _():
            value(k)
            for r in range(EARLY, cuts):
                x_start(r)

        return carry

    lax.fori_loop(ready, groups, value_loop, 0)

    def settle(c, carry):
        other = remote(place(c, 1 - core), place(c, 1 - core), f_ss.at[c], f_rs.at[c], sibling, f)
        other.wait_recv()
        final_copy(c).wait_send()

        @pl.when(z < depth - 1)
        def _():
            right_copy(c).wait_send()

        @pl.when(z > 0)
        def _():
            left_copy(c).wait_send()

        return carry

    def tidy():
        for i in range(groups):
            dk_out[0, :, i * HEAD_SIZE : (i + 1) * HEAD_SIZE] = collect(
                dk_own, dk_recv, dk_send, dk_ss, dk_rs, i
            )

        @pl.when(has_next)
        def _():
            v_copy(1).wait_send()
            for i in range(groups):
                k_copy(1, i).wait_send()

        @pl.when(s + 2 < n_s)
        def _():
            for i in range(groups):
                k_copy(2, i).wait_send()

        @pl.when(even_two)
        def _():
            v_copy(2).wait_send()

        @pl.when(relays)
        def _():
            v_relay().wait_send()

        for d in range(1, BACK + 1):
            @pl.when(s >= d)
            def _():
                for i in range(groups):
                    back_copy(dv_send, dv_recv, dv_ss, dv_rs, d, i).wait_send()
                    back_copy(dk_send, dk_recv, dk_ss, dk_rs, d, i).wait_send()
        for j in peers:
            for r in range(cuts):
                x_copy(r, j).wait_send()
            for i in range(groups):
                vg_copy(i, j).wait_send()
        for u in range(units):
            pair_copy(u).wait_send()

    shift = jnp.minimum(SLACK * (depth - 1 - z), SLACK * z + LATER)

    def second_loop(i, carry):
        second_pass(i)
        return carry

    total = chunks + SLACK * (depth - 1) + LATER
    parts = heads // PAIR

    def line(t, carry):
        own = t - shift
        u = own // SUBS

        @pl.when(jnp.logical_and(own % SUBS == 0, jnp.logical_and(own >= 0, u < units)))
        def _():
            pair_copy(u).wait_recv()
            w_own[u] = w_own[u] + pair_recv[u].astype(F32)

        step(t, carry)

        @pl.when(jnp.logical_and(own % SUBS == 0, jnp.logical_and(own >= 0, u + AHEAD < units)))
        def _():
            weight_unit(u + AHEAD)

        behind = jnp.minimum(t - SLACK * z - LATER, t - SLACK * (depth - 1 - z)) - BEHIND

        @pl.when(jnp.logical_and(behind >= 0, behind < chunks - BEHIND))
        def _():
            settle(behind, 0)

        @pl.when(t == total - BEHIND)
        def _():
            tidy()

        @pl.when(jnp.logical_and(own == chunks - 1, last))
        def _():
            lax.fori_loop(early, groups, second_loop, 0)

        piece = (own - FROM) // EVERY
        turn = jnp.logical_and(own >= FROM, (own - FROM) % EVERY == 0)

        @pl.when(jnp.logical_and(jnp.logical_and(turn, z == depth - 2), piece < HELD * parts))
        def _():
            second_piece(groups - HELD + piece // parts, piece % parts)

        return carry

    for u in range(AHEAD):
        weight_unit(u)
    lax.fori_loop(jnp.where(z < depth - 2, groups - 1, groups), groups, second_loop, 0)
    lax.fori_loop(0, total, line, 0)

    lax.fori_loop(chunks - BEHIND, chunks, settle, 0)


def settle_outputs(*refs):
    sources, outs, sems = refs[:4], refs[4:8], refs[8]
    saves = [pltpu.make_async_copy(sources[i], outs[i], sems.at[i]) for i in range(4)]
    for save in saves:
        save.start()
    for save in saves:
        save.wait()


def shards(n_s, n_f, layer_inputs, queries, key_states, value_states, output_gradient, doc_blocks):
    rows = queries.shape[1]
    kvw = key_states.shape[2]
    groups = kvw // HEAD_SIZE
    heads = queries.shape[2] // kvw
    width = layer_inputs.shape[2] // n_f
    cuts = 4 if width % (4 * 128) == 0 else 2
    cut = width // cuts
    units = cuts * (groups // 2)
    chunks = units * SUBS
    keys = (BACK + 1) * rows
    V = pltpu.VMEM
    D = pltpu.SemaphoreType.DMA
    strip = V((chunks, cut // SUBS, HEAD_SIZE), BF16)
    scratch = [
        V((rows, queries.shape[2]), BF16),
        V((rows, queries.shape[2]), BF16),
        V((BACK + 1, rows, kvw), BF16),
        V((BACK + 1, rows, kvw), BF16),
        V((cuts, n_f, rows, cut), BF16),
        V((groups, heads // PAIR, keys, PAIR * rows), F32),
        V((keys, PAIR * rows), F32),
        V((rows, kvw), F32),
        V((BACK, rows, kvw), BF16),
        V((BACK, rows, kvw), BF16),
        V((rows, kvw), F32),
        V((BACK, rows, kvw), BF16),
        V((BACK, rows, kvw), BF16),
        V((n_f, rows, kvw), BF16),
        V((units, cut, HEAD_SIZE), F32),
        V((units, cut, HEAD_SIZE), BF16),
        V((units, cut, HEAD_SIZE), BF16),
        strip, strip, strip, strip,
        pltpu.SMEM(doc_blocks.shape, jnp.int32),
        D((5,)), D((cuts,)),
        D((BACK, groups)), D((BACK, groups)),
        D((BACK,)), D((BACK,)), D((1,)), D((cuts, n_f)), D((cuts, n_f)),
        D((BACK, groups)), D((BACK, groups)), D((BACK, groups)), D((BACK, groups)),
        D((groups, n_f)), D((groups, n_f)), D((units,)), D((units,)),
        D((chunks,)), D((chunks,)), D((chunks,)), D((chunks,)), D((chunks,)), D((chunks,)),
        V((keys, HEAD_SIZE), F32),
    ]
    far = pl.BlockSpec(memory_space=pltpu.HBM)
    near = pl.BlockSpec(memory_space=pltpu.VMEM)
    out_shape = [
        jax.ShapeDtypeStruct(queries.shape, BF16),
        jax.ShapeDtypeStruct(key_states.shape, BF16),
        jax.ShapeDtypeStruct(key_states.shape, BF16),
        jax.ShapeDtypeStruct((width, kvw), BF16),
    ]
    held = [
        pltpu.with_memory_space_constraint(a, pltpu.HBM)
        for a in (doc_blocks, layer_inputs, queries, key_states, value_states, output_gradient)
    ]
    made = pl.pallas_call(
        functools.partial(kernel, n_s, n_f, groups, heads, cuts),
        out_shape=[pltpu.VMEM(o.shape, o.dtype) for o in out_shape],
        in_specs=[far] * 6,
        out_specs=[near] * 4,
        scratch_shapes=scratch,
        compiler_params=pltpu.CompilerParams(
            collective_id=0, has_side_effects=True, vmem_limit_bytes=VMEM_LIMIT
        ),
    )(*held)
    return tuple(
        pl.pallas_call(
            settle_outputs,
            out_shape=out_shape,
            in_specs=[near] * 4,
            out_specs=[far] * 4,
            scratch_shapes=[D((4,))],
            compiler_params=pltpu.CompilerParams(vmem_limit_bytes=SMALL_LIMIT),
        )(*made)
    )


def solution(mesh):
    sizes = dict(mesh.shape)
    return jax.shard_map(
        functools.partial(shards, sizes["seq"], sizes["fsdp"]),
        mesh=mesh,
        in_specs=(P("fsdp", "seq", None),) * 5 + (P("fsdp", None),),
        out_specs=(P("fsdp", "seq", None),) * 3 + (P("fsdp", None),),
        check_vma=False,
    )
```
